128 devices in a mesh: tile: 8 (over x_hi, z), src: 16 (over y, x_lo, core).
Axes of the slice: x: 4 (x_hi: 2, x_lo: 2; x = x_hi * 2 + x_lo), y: 4, z: 4, core: 2. Of those that a mesh axis runs over, the one named last changes fastest.
Arguments:
- permittivity: float32 [128, 16, 320], P(('tile', 'src')), may hold values from 1 to 2
- e_start: float32 [16, 3, 128, 16, 320], P('src', None, 'tile'), may hold values from -6 to 6
- h_start: float32 [16, 3, 128, 16, 320], P('src', None, 'tile'), may hold values from -6 to 6
- e_cotangent: float32 [16, 3, 128, 16, 320], P('src', None, 'tile'), may hold values from -6 to 6
- h_cotangent: float32 [16, 3, 128, 16, 320], P('src', None, 'tile'), may hold values from -6 to 6
Outputs:
- e_final: float32 [16, 3, 128, 16, 320], P('src', None, 'tile')
- gradient: float32 [128, 16, 320], P(('tile', 'src'))
The draws below stay inside these ranges and needn't reach their ends.
All inputs are finite; a program needn't handle non-finite values.
Results may differ from the reference program's by a relative error of at most 0.00002.
Values sent between devices are 32-bit elements; how exact they have to be, the bound alone decides.
No kernel may reach another device: no remote copies, remote signals or barrier semaphores. Data moves between devices by JAX's collectives and lax.ppermute only.
A program may use at most 64 MiB of HBM per device.

```python
import math
import jax
import jax.numpy as jnp
from jax import lax

NY = 16
NZ = 320
STEPS = 6
SOURCES = 16
NX = 128


def spiked(array, key, source, target, parts, factor):
    def block_of(dim):
        return (jnp.arange(array.shape[dim]) // (array.shape[dim] // parts)).reshape((-1,) + (1,) * (array.ndim - 1 - dim))

    near = jax.random.permutation(key, parts)[block_of(target)]
    far = (block_of(target) + parts // 2) % parts
    return jnp.where((block_of(source) == near) | (block_of(source) == far), factor * array, array)


def shard_levels(stream_key, shape, shards, smallest, high):
    factor_of, own = 1.0, jax.random.fold_in(stream_key, 6)
    for position, shards_of in shards:
        heights = jnp.exp(jax.random.uniform(jax.random.fold_in(own, position), (shards_of,), jnp.float32, smallest / len(shards), high / len(shards)))
        factor_of = factor_of * jnp.repeat(heights, shape[position] // shards_of).reshape([-1 if axis == position else 1 for axis in range(len(shape))])
    return factor_of


def gaussian(stream_key, shape, scale, reach, cuts=(), dtype=jnp.bfloat16):
    drawn = jax.random.normal(stream_key, shape, jnp.float32) * scale
    if len(cuts) > 0:
        drawn = shard_levels(stream_key, shape, cuts, -0.22, 0.18) * drawn
    return jnp.clip(drawn, min=-reach, max=reach).astype(dtype)


def heavy_noise(stream_key, extent, scale, most, pieces, heavy, kind=jnp.bfloat16):
    result = scale * jax.random.normal(stream_key, extent, jnp.float32)
    if pieces:
        result = result * shard_levels(stream_key, extent, pieces, -0.22, 0.18)
    return jnp.clip(spiked(result, jax.random.fold_in(stream_key, 3), *heavy), -most, most).astype(kind)


def setup_inputs(seed: int = 0) -> dict:
    key_of = jax.random.split(jax.random.key(seed), 6)
    permittivity = jnp.clip(jnp.exp(math.log(2.0) - 0.6931472 * jax.random.uniform(key_of[0], (NX, NY, NZ), jnp.float32) ** shard_levels(key_of[0], (NX, NY, NZ), ((0, 128),), -0.2, 0.2)), 1.0, 2.0)
    e_start = gaussian(key_of[1], (SOURCES, 3, NX, NY, NZ), 1.0, 6.0, ((0, 16), (2, 8)), jnp.float32)
    h_start = gaussian(key_of[2], (SOURCES, 3, NX, NY, NZ), 1.0, 6.0, ((0, 16), (2, 8)), jnp.float32)
    e_cotangent = heavy_noise(key_of[3], (SOURCES, 3, NX, NY, NZ), 1.0, 6.0, ((0, 16), (2, 8)), (0, 2, 16, 2.0), jnp.float32)
    h_cotangent = gaussian(key_of[4], (SOURCES, 3, NX, NY, NZ), 1.0, 6.0, ((0, 16), (2, 8)), jnp.float32)
    return dict(permittivity=permittivity, e_start=e_start, h_start=h_start, e_cotangent=e_cotangent, h_cotangent=h_cotangent)


courant = 0.57

def ahead(field, axis):
    size = field.shape[axis]
    upper = lax.slice_in_dim(field, 1, size, axis=axis)
    zeros = jnp.zeros_like(lax.slice_in_dim(field, 0, 1, axis=axis))
    return jnp.concatenate([upper, zeros], axis) - field

def behind(field, axis):
    size = field.shape[axis]
    lower = lax.slice_in_dim(field, 0, size - 1, axis=axis)
    zeros = jnp.zeros_like(lax.slice_in_dim(field, 0, 1, axis=axis))
    return field - jnp.concatenate([zeros, lower], axis)

def curl_with(field, differ):
    return jnp.stack([differ(field[2], 1) - differ(field[1], 2), differ(field[0], 2) - differ(field[2], 0), differ(field[1], 0) - differ(field[0], 1)])

def leapfrog(inverse, efield, hfield):
    for turn in range(STEPS):
        hfield = hfield - courant * curl_with(efield, ahead)
        efield = efield + courant * inverse * curl_with(hfield, behind)
    return (efield, hfield)

def reference(permittivity, e_start, h_start, e_cotangent, h_cotangent):

    def per_source(total, items):
        efield, hfield, e_cot, h_cot = items
        outputs, pullback = jax.vjp(lambda perm: leapfrog(1.0 / perm, efield, hfield), permittivity)
        grad_perm, = pullback((e_cot, h_cot))
        return (total + grad_perm, outputs[0])
    start = jnp.zeros(permittivity.shape, jnp.float32)
    gradient, e_final = lax.scan(per_source, start, (e_start, h_start, e_cotangent, h_cotangent))
    return (e_final, gradient)
```

```python
import jax
import jax.numpy as jnp
from jax import lax
from jax.experimental import pallas as pl
from jax.experimental.pallas import tpu as pltpu
from jax.sharding import PartitionSpec as P

STEPS = 6
courant = 0.57
NX, NY, NZ = 16, 16, 320
WIDE = 384
GHOST = 6
ALL = NX + 2 * GHOST


F32 = jnp.float32


def plane_list(depth, upward):
    if upward:
        return [(a, c, p) for p in range(NX - depth, NX) for a in range(2) for c in range(3)]
    whole = [(a, c, p) for p in range(depth - 1) for a in range(2) for c in range(3)]
    return whole + [(0, 1, depth - 1), (0, 2, depth - 1)]


def pack_body(depth, e_ref, h_ref, up_ref, dn_ref):
    arrays = (e_ref, h_ref)
    for upward, out in ((True, up_ref), (False, dn_ref)):
        planes = plane_list(depth, upward)
        for k in range(len(planes) // 2):
            tails = []
            for j in range(2):
                a, c, p = planes[2 * k + j]
                x = arrays[a][0, c, p]
                out[k, 2 * j] = x[:, 0:128]
                out[k, 2 * j + 1] = x[:, 128:256]
                tails.append(x[:, 256:320])
            out[k, 4] = jnp.concatenate(tails, axis=1)


def pack(depth, e, h, name):
    up = len(plane_list(depth, True)) // 2
    dn = len(plane_list(depth, False)) // 2
    return pl.pallas_call(
        lambda *refs: pack_body(depth, *refs),
        out_shape=(
            jax.ShapeDtypeStruct((up, 5, 16, 128), F32),
            jax.ShapeDtypeStruct((dn, 5, 16, 128), F32),
        ),
        in_specs=[pl.BlockSpec(memory_space=pltpu.VMEM)] * 2,
        out_specs=[pl.BlockSpec(memory_space=pltpu.VMEM)] * 2,
        compiler_params=pltpu.CompilerParams(vmem_limit_bytes=16 << 20),
        name=name,
    )(e, h)


def unpack(depth, buf, upward, put):
    planes = plane_list(depth, upward)
    for k in range(len(planes) // 2):
        tail = buf[k, 4]
        low = lax.broadcasted_iota(jnp.int32, (16, 128), 1) < 64
        tails = (jnp.where(low, tail, 0.0), jnp.where(low, pltpu.roll(tail, 64, 1), 0.0))
        for j in range(2):
            a, c, p = planes[2 * k + j]
            place = p - NX + GHOST if upward else p + NX + GHOST
            put(a, c, place, (buf[k, 2 * j], buf[k, 2 * j + 1], tails[j]))


def widen(x):
    return (x[:, 0:128], x[:, 128:256], jnp.concatenate([x[:, 256:320], jnp.zeros((16, 64), F32)], axis=1))


def store(ref, index, tiles):
    for k in range(3):
        ref[(*index, slice(None), slice(128 * k, 128 * k + 128))] = tiles[k]


def tiles_of(x):
    return [[x[8 * r : 8 * r + 8, 128 * k : 128 * k + 128] for k in range(3)] for r in range(2)]


def joined(v):
    return jnp.concatenate([jnp.concatenate(row, axis=1) for row in v], axis=0)


class Shifts:
    def __init__(self):
        lane = lax.broadcasted_iota(jnp.int32, (8, 128), 1)
        row = lax.broadcasted_iota(jnp.int32, (8, 128), 0)
        self.first_lane, self.last_lane = lane == 0, lane == 127
        self.first_row, self.last_row = row == 0, row == 7

    def ahead_z(self, v):
        out = []
        for r in range(2):
            m = [pltpu.roll(t, 127, 1) for t in v[r]]
            out.append([jnp.where(self.last_lane, m[1], m[0]), jnp.where(self.last_lane, m[2], m[1]), m[2]])
        return out

    def behind_z(self, v):
        out = []
        for r in range(2):
            m = [pltpu.roll(t, 1, 1) for t in v[r]]
            out.append([jnp.where(self.first_lane, 0.0, m[0])] + [jnp.where(self.first_lane, m[k - 1], m[k]) for k in (1, 2)])
        return out

    def ahead_y(self, v):
        m = [[pltpu.roll(t, 7, 0) for t in row] for row in v]
        return [
            [jnp.where(self.last_row, m[1][k], m[0][k]) for k in range(3)],
            [jnp.where(self.last_row, 0.0, m[1][k]) for k in range(3)],
        ]

    def behind_y(self, v):
        m = [[pltpu.roll(t, 1, 0) for t in row] for row in v]
        return [
            [jnp.where(self.first_row, 0.0, m[0][k]) for k in range(3)],
            [jnp.where(self.first_row, m[0][k], m[1][k]) for k in range(3)],
        ]


def each(fn, *vs):
    return [[fn(*(v[r][k] for v in vs)) for k in range(3)] for r in range(2)]


def new_h(sh, e, e1n, e2n, h):
    y2, y0 = sh.ahead_y(e[2]), sh.ahead_y(e[0])
    z1, z0 = sh.ahead_z(e[1]), sh.ahead_z(e[0])
    h0 = each(lambda h, a, b, c, d: h - ((a - b) - (c - d)), h[0], y2, e[2], z1, e[1])
    h1 = each(lambda h, a, b, c, d: h - ((a - b) - (c - d)), h[1], z0, e[0], e2n, e[2])
    h2 = each(lambda h, a, b, c, d: h - ((a - b) - (c - d)), h[2], e1n, e[1], y0, e[0])
    return h0, h1, h2


def curl_behind(sh, h, h1p, h2p):
    y2, y0 = sh.behind_y(h[2]), sh.behind_y(h[0])
    z1, z0 = sh.behind_z(h[1]), sh.behind_z(h[0])
    f = lambda a, b, c, d: (a - b) - (c - d)
    return (
        each(f, h[2], y2, h[1], z1),
        each(f, h[0], z0, h[2], h2p),
        each(f, h[1], h1p, h[0], y0),
    )


def put_h(h_ref, p, h):
    for c in range(3):
        h_ref[c, p] = joined(h[c])


def step_plane(sh, e_at, e_put, h_ref, ci_ref, p, use):
    e = [tiles_of(e_at(c, p)) for c in range(3)]
    e1n, e2n = tiles_of(e_at(1, p + 1)), tiles_of(e_at(2, p + 1))
    h = new_h(sh, e, e1n, e2n, [tiles_of(h_ref[c, p]) for c in range(3)])
    put_h(h_ref, p, h)
    curl = curl_behind(sh, h, tiles_of(h_ref[1, p - 1]), tiles_of(h_ref[2, p - 1]))
    ci = tiles_of(ci_ref[p])
    for c in range(3):
        e_put(c, p, joined(each(lambda x, k, y: x + k * y, e[c], ci, curl[c])))
    use(p, curl)


def first_plane(sh, e_at, h_ref, p):
    e = [tiles_of(e_at(c, p)) for c in range(3)]
    e1n, e2n = tiles_of(e_at(1, p + 1)), tiles_of(e_at(2, p + 1))
    put_h(h_ref, p, new_h(sh, e, e1n, e2n, [tiles_of(h_ref[c, p]) for c in range(3)]))


def sweep(sh, tile, reach, e_at, e_put, h_ref, ci_ref, use):
    nothing = lambda p, curl: None

    @pl.when(tile > 0)
    def _():
        first_plane(sh, e_at, h_ref, GHOST - reach)

        @pl.loop(GHOST - reach + 1, GHOST)
        def _(p):
            step_plane(sh, e_at, e_put, h_ref, ci_ref, p, nothing)

    @pl.loop(GHOST, GHOST + NX)
    def _(p):
        step_plane(sh, e_at, e_put, h_ref, ci_ref, p, use)

    @pl.loop(GHOST + NX, GHOST + NX + reach - 1)
    def _(p):
        step_plane(sh, e_at, e_put, h_ref, ci_ref, p, nothing)


def fill_inverse(perm_ref, ci_ref):
    places = [(s, 0, GHOST + s) for s in range(NX)]
    places += [(s, 1, GHOST + NX + s) for s in range(GHOST - 1)]
    places += [(s, 1, s - NX + GHOST) for s in range(NX - GHOST + 1, NX)]
    for s, which, place in places:
        t = widen(perm_ref[s, which])
        store(ci_ref, (place,), [jnp.where(x > 0, (courant * courant) / jnp.where(x > 0, x, 1.0), 0.0) for x in t])


def adjoint_body(tile_ref, perm_ref, a_ref, b_ref, up_ref, dn_ref, hist_ref, ci_ref, h_ref, e_ref, sem):
    sh = Shifts()
    tile = tile_ref[0]
    depth = STEPS - 1
    fill_inverse(perm_ref, ci_ref)

    def put(a, c, place, t):
        if a == 1:
            store(h_ref, (c, place), [x * (-1.0 / courant) for x in t])
        else:
            ci = ci_ref[place]
            store(e_ref, (0, c, place), [t[k] * ci[:, 128 * k : 128 * k + 128] * (1.0 / (courant * courant)) for k in range(3)])

    for c in range(3):
        @pl.loop(0, NX)
        def _(p):
            put(0, c, p + GHOST, widen(a_ref[0, c, p]))
            put(1, c, p + GHOST, widen(b_ref[0, c, p]))
    unpack(depth, up_ref, True, put)
    unpack(depth, dn_ref, False, put)

    def out(j):
        return pltpu.make_async_copy(e_ref.at[j, :, pl.ds(GHOST, NX)], hist_ref.at[j], sem.at[j])

    out(0).start()
    for j in range(depth):
        def e_put(c, p, x, j=j):
            e_ref[j + 1, c, p] = x

        sweep(sh, tile, depth - j, lambda c, p, j=j: e_ref[j, c, p], e_put, h_ref, ci_ref, lambda p, curl: None)
        out(j + 1).start()
    for j in range(depth + 1):
        out(j).wait()


def forward_body(tile_ref, perm_ref, e0_ref, h0_ref, up_ref, dn_ref, hist_ref, efin_ref, sum_ref, ci_ref, h_ref, e_ref, ahat_ref, sem):
    sh = Shifts()
    tile = tile_ref[0]
    depth = STEPS

    def fetch(j):
        return pltpu.make_async_copy(hist_ref.at[j], ahat_ref.at[j], sem.at[j])

    for t in range(STEPS):
        fetch(STEPS - 1 - t).start()
    fill_inverse(perm_ref, ci_ref)

    def put(a, c, place, t):
        if a == 1:
            store(h_ref, (c, place), [x * (1.0 / courant) for x in t])
        else:
            store(e_ref, (c, place), t)

    for c in range(3):
        @pl.loop(0, NX)
        def _(p):
            put(0, c, p + GHOST, widen(e0_ref[0, c, p]))
            put(1, c, p + GHOST, widen(h0_ref[0, c, p]))
    unpack(depth, up_ref, True, put)
    unpack(depth, dn_ref, False, put)

    def e_put(c, p, x):
        e_ref[c, p] = x

    for t in range(STEPS):
        fetch(STEPS - 1 - t).wait()

        def use(p, curl, t=t):
            q = p - GHOST
            a = [tiles_of(ahat_ref[STEPS - 1 - t, c, q]) for c in range(3)]
            s = each(lambda x0, y0, x1, y1, x2, y2: x0 * y0 + x1 * y1 + x2 * y2, a[0], curl[0], a[1], curl[1], a[2], curl[2])
            s = joined(s)
            if t > 0:
                s = s + sum_ref[q]
            sum_ref[q] = s

        sweep(sh, tile, depth - t, lambda c, p: e_ref[c, p], e_put, h_ref, ci_ref, use)
    for c in range(3):
        @pl.loop(0, NX)
        def _(p):
            efin_ref[0, c, p] = e_ref[c, p + GHOST][:, :NZ]


VM = pl.BlockSpec(memory_space=pltpu.VMEM)
SM = pl.BlockSpec(memory_space=pltpu.SMEM)
ANY = pl.BlockSpec(memory_space=pl.ANY)
FIELD = (3, ALL, NY, WIDE)


def adjoint(tile, perm, a, b, up, dn, interpret=False):
    return pl.pallas_call(
        adjoint_body,
        out_shape=jax.ShapeDtypeStruct((STEPS, 3, NX, NY, WIDE), F32),
        in_specs=[SM, VM, VM, VM, VM, VM],
        out_specs=ANY,
        scratch_shapes=[
            pltpu.VMEM((ALL, NY, WIDE), F32),
            pltpu.VMEM(FIELD, F32),
            pltpu.VMEM((STEPS, *FIELD), F32),
            pltpu.SemaphoreType.DMA((STEPS,)),
        ],
        compiler_params=pltpu.CompilerParams(vmem_limit_bytes=36 << 20),
        name="adjoint",
        interpret=interpret,
    )(tile, perm, a, b, up, dn)


def forward(tile, perm, e, h, up, dn, hist, interpret=False):
    return pl.pallas_call(
        forward_body,
        out_shape=(
            jax.ShapeDtypeStruct((1, 3, NX, NY, NZ), F32),
            jax.ShapeDtypeStruct((NX, NY, WIDE), F32),
        ),
        in_specs=[SM, VM, VM, VM, VM, VM, ANY],
        out_specs=(VM, VM),
        scratch_shapes=[
            pltpu.VMEM((ALL, NY, WIDE), F32),
            pltpu.VMEM(FIELD, F32),
            pltpu.VMEM(FIELD, F32),
            pltpu.VMEM((STEPS, 3, NX, NY, WIDE), F32),
            pltpu.SemaphoreType.DMA((STEPS,)),
        ],
        compiler_params=pltpu.CompilerParams(vmem_limit_bytes=36 << 20),
        name="forward",
        interpret=interpret,
    )(tile, perm, e, h, up, dn, hist)


def on_device(permittivity, e_start, h_start, e_cotangent, h_cotangent):
    tiles, sources = lax.axis_size("tile"), lax.axis_size("src")
    tile = lax.axis_index("tile").astype(jnp.int32).reshape(1)
    upward = [(i, i + 1) for i in range(tiles - 1)]
    downward = [(i + 1, i) for i in range(tiles - 1)]
    near = [(t * sources + s, (t - 1) * sources + s) for t in range(1, tiles) for s in range(GHOST - 1)]
    near += [(t * sources + s, (t + 1) * sources + s) for t in range(tiles - 1) for s in range(NX - GHOST + 1, NX)]

    border = lax.ppermute(permittivity, ("tile", "src"), near)
    a_up, a_dn = pack(STEPS - 1, e_cotangent, h_cotangent, "pack_adjoint")
    a_up = lax.ppermute(a_up, "tile", upward)
    a_dn = lax.ppermute(a_dn, "tile", downward)
    e_up, e_dn = pack(STEPS, e_start, h_start, "pack_forward")
    e_up = lax.ppermute(e_up, "tile", upward)
    e_dn = lax.ppermute(e_dn, "tile", downward)
    both = jnp.concatenate([permittivity, border], axis=0)
    perm = lax.all_to_all(jnp.broadcast_to(both, (sources, *both.shape)), "src", 0, 0, tiled=True)
    hist = adjoint(tile, perm, e_cotangent, h_cotangent, a_up, a_dn)
    e_final, sums = forward(tile, perm, e_start, h_start, e_up, e_dn, hist)
    parts = lax.all_to_all(sums, "src", 0, 0, tiled=True)
    total = jnp.sum(parts, axis=0, keepdims=True)[:, :, :NZ]
    gradient = -(courant * courant) * total / permittivity
    return e_final, gradient


def solution(mesh):
    field = P("src", None, "tile", None, None)
    in_specs = (P(("tile", "src"), None, None), field, field, field, field)
    out_specs = (field, P(("tile", "src"), None, None))
    return jax.shard_map(on_device, mesh=mesh, in_specs=in_specs, out_specs=out_specs, check_vma=False)
```

```python
import jax
import jax.numpy as jnp
from jax import lax
from jax.experimental import pallas as pl
from jax.experimental.pallas import tpu as pltpu
from jax.sharding import PartitionSpec as P

STEPS = 6
courant = 0.57
NX, NY, NZ = 16, 16, 320
WIDE = 384
DEEP = 6
GHOST = 12
ALL = GHOST + NX + 12


F32 = jnp.float32


def plane_list(depth, upward):
    if upward:
        return [(a, c, p) for p in range(NX - depth, NX) for a in range(2) for c in range(3)]
    whole = [(a, c, p) for p in range(depth - 1) for a in range(2) for c in range(3)]
    return whole + [(0, 1, depth - 1), (0, 2, depth - 1)]


def pack_body(depth, e_ref, h_ref, up_ref, dn_ref):
    arrays = (e_ref, h_ref)
    for upward, out in ((True, up_ref), (False, dn_ref)):
        planes = plane_list(depth, upward)
        for k in range(len(planes) // 2):
            tails = []
            for j in range(2):
                a, c, p = planes[2 * k + j]
                x = arrays[a][0, c, p]
                out[k, 2 * j] = x[:, 0:128]
                out[k, 2 * j + 1] = x[:, 128:256]
                tails.append(x[:, 256:320])
            out[k, 4] = jnp.concatenate(tails, axis=1)


def pack(depth, e, h, name):
    up = len(plane_list(depth, True)) // 2
    dn = len(plane_list(depth, False)) // 2
    return pl.pallas_call(
        lambda *refs: pack_body(depth, *refs),
        out_shape=(
            jax.ShapeDtypeStruct((up, 5, 16, 128), F32),
            jax.ShapeDtypeStruct((dn, 5, 16, 128), F32),
        ),
        in_specs=[pl.BlockSpec(memory_space=pltpu.VMEM)] * 2,
        out_specs=[pl.BlockSpec(memory_space=pltpu.VMEM)] * 2,
        compiler_params=pltpu.CompilerParams(vmem_limit_bytes=16 << 20),
        name=name,
    )(e, h)


def unpack(depth, buf, upward, put):
    planes = plane_list(depth, upward)
    for k in range(len(planes) // 2):
        tail = buf[k, 4]
        low = lax.broadcasted_iota(jnp.int32, (16, 128), 1) < 64
        tails = (jnp.where(low, tail, 0.0), jnp.where(low, pltpu.roll(tail, 64, 1), 0.0))
        for j in range(2):
            a, c, p = planes[2 * k + j]
            place = p - NX + GHOST if upward else p + NX + GHOST
            put(a, c, place, (buf[k, 2 * j], buf[k, 2 * j + 1], tails[j]))


def widen(x):
    return (x[:, 0:128], x[:, 128:256], jnp.concatenate([x[:, 256:320], jnp.zeros((16, 64), F32)], axis=1))


def store(ref, index, tiles):
    for k in range(3):
        ref[(*index, slice(None), slice(128 * k, 128 * k + 128))] = tiles[k]


def tiles_of(x):
    return [[x[8 * r : 8 * r + 8, 128 * k : 128 * k + 128] for k in range(3)] for r in range(2)]


def joined(v):
    return jnp.concatenate([jnp.concatenate(row, axis=1) for row in v], axis=0)


class Shifts:
    def __init__(self):
        lane = lax.broadcasted_iota(jnp.int32, (8, 128), 1)
        row = lax.broadcasted_iota(jnp.int32, (8, 128), 0)
        self.first_lane, self.last_lane = lane == 0, lane == 127
        self.first_row, self.last_row = row == 0, row == 7

    def ahead_z(self, v):
        out = []
        for r in range(2):
            m = [pltpu.roll(t, 127, 1) for t in v[r]]
            out.append([jnp.where(self.last_lane, m[1], m[0]), jnp.where(self.last_lane, m[2], m[1]), m[2]])
        return out

    def behind_z(self, v):
        out = []
        for r in range(2):
            m = [pltpu.roll(t, 1, 1) for t in v[r]]
            out.append([jnp.where(self.first_lane, 0.0, m[0])] + [jnp.where(self.first_lane, m[k - 1], m[k]) for k in (1, 2)])
        return out

    def ahead_y(self, v):
        m = [[pltpu.roll(t, 7, 0) for t in row] for row in v]
        return [
            [jnp.where(self.last_row, m[1][k], m[0][k]) for k in range(3)],
            [jnp.where(self.last_row, 0.0, m[1][k]) for k in range(3)],
        ]

    def behind_y(self, v):
        m = [[pltpu.roll(t, 1, 0) for t in row] for row in v]
        return [
            [jnp.where(self.first_row, 0.0, m[0][k]) for k in range(3)],
            [jnp.where(self.first_row, m[0][k], m[1][k]) for k in range(3)],
        ]


def each(fn, *vs):
    return [[fn(*(v[r][k] for v in vs)) for k in range(3)] for r in range(2)]


def h_phase(sh, e_at, h_ref, ez_ref, hz_ref, q):
    e = [[tiles_of(e_at(c, q + d)) for c in range(3)] for d in range(2)]
    e.append([None] + [tiles_of(e_at(c, q + 2)) for c in (1, 2)])
    for d in range(2):
        here, then = e[d], e[d + 1]
        z0, z1 = (tiles_of(ez_ref[c, q + d]) for c in range(2))
        y2, y0 = sh.ahead_y(here[2]), sh.ahead_y(here[0])
        h = [tiles_of(h_ref[c, q + d]) for c in range(3)]
        f = lambda h, a, b, c, d: h - ((a - b) - (c - d))
        h = (
            each(f, h[0], y2, here[2], z1, here[1]),
            each(f, h[1], z0, here[0], then[2], here[2]),
            each(f, h[2], then[1], here[1], y0, here[0]),
        )
        for c in range(3):
            h_ref[c, q + d] = joined(h[c])
        for c in range(2):
            hz_ref[c, q + d] = joined(sh.behind_z(h[c]))


def e_phase(sh, e_at, e_put, h_ref, hz_ref, ci_ref, q, use):
    before = [None] + [tiles_of(h_ref[c, q - 1]) for c in (1, 2)]
    f = lambda a, b, c, d: (a - b) - (c - d)
    for d in range(2):
        h = [tiles_of(h_ref[c, q + d]) for c in range(3)]
        z0, z1 = (tiles_of(hz_ref[c, q + d]) for c in range(2))
        y2, y0 = sh.behind_y(h[2]), sh.behind_y(h[0])
        curl = (
            each(f, h[2], y2, h[1], z1),
            each(f, h[0], z0, h[2], before[2]),
            each(f, h[1], before[1], h[0], y0),
        )
        ci = tiles_of(ci_ref[q + d])
        for c in range(3):
            e_put(c, q + d, joined(each(lambda x, k, y: x + k * y, tiles_of(e_at(c, q + d)), ci, curl[c])))
        if use is not None:
            use(q + d, curl)
        before = h


def sweep(sh, tile, reach, e_at, e_put, e_mirror, h_ref, ez_ref, hz_ref, ci_ref, use):
    @pl.when(tile == 0)
    def _():
        for c in (1, 2):
            e_mirror(c)

    def turn(q, fn):
        for d in range(2):
            for c in range(2):
                ez_ref[c, q + 2 + d] = joined(sh.ahead_z(tiles_of(e_at(c, q + 2 + d))))
        h_phase(sh, e_at, h_ref, ez_ref, hz_ref, q)
        e_phase(sh, e_at, e_put, h_ref, hz_ref, ci_ref, q - 2, fn)

    even = reach + reach % 2
    own, end = GHOST, GHOST + NX
    ranges = ((own - even - 2, own + 2, None), (own + 2, end + 2, use), (end + 2, GHOST + NX + reach - 1 + reach % 2 * 1 + 2, None))
    ranges = ranges[:2] + ((end + 2, end + even + 2 if reach % 2 == 0 else end + reach + 1, None),)
    for start, stop, fn in ranges:
        if stop > start:
            @pl.loop(0, (stop - start) // 2)
            def _(i, start=start, fn=fn):
                turn(start + 2 * i, fn)


def fill_inverse(perm_ref, ci_ref):
    places = [(s, 0, GHOST + s) for s in range(NX)]
    places += [(s, 1, GHOST + NX + s) for s in range(DEEP - 1)]
    places += [(s, 1, s - NX + GHOST) for s in range(NX - DEEP + 1, NX)]
    for s, which, place in places:
        t = widen(perm_ref[s, which])
        store(ci_ref, (place,), [jnp.where(x > 0, (courant * courant) / jnp.where(x > 0, x, 1.0), 0.0) for x in t])


def adjoint_body(tile_ref, perm_ref, a_ref, b_ref, up_ref, dn_ref, hist_ref, ci_ref, h_ref, e_ref, ez_ref, hz_ref, sem):
    sh = Shifts()
    tile = tile_ref[0]
    depth = STEPS - 1
    fill_inverse(perm_ref, ci_ref)

    def put(a, c, place, t):
        if a == 1:
            store(h_ref, (c, place), [x * (-1.0 / courant) for x in t])
        else:
            ci = ci_ref[place]
            store(e_ref, (0, c, place), [t[k] * ci[:, 128 * k : 128 * k + 128] * (1.0 / (courant * courant)) for k in range(3)])

    for c in range(3):
        @pl.loop(0, NX)
        def _(p):
            put(0, c, p + GHOST, widen(a_ref[0, c, p]))
            put(1, c, p + GHOST, widen(b_ref[0, c, p]))
    unpack(depth, up_ref, True, put)
    unpack(depth, dn_ref, False, put)

    def out(j):
        return pltpu.make_async_copy(e_ref.at[j, :, pl.ds(GHOST, NX)], hist_ref.at[j], sem.at[j])

    out(0).start()
    for j in range(depth):
        def e_put(c, p, x, j=j):
            e_ref[j + 1, c, p] = x

        def e_mirror(c, j=j):
            e_ref[j, c, GHOST - 1] = e_ref[j, c, GHOST]

        sweep(sh, tile, depth - j, lambda c, p, j=j: e_ref[j, c, p], e_put, e_mirror, h_ref, ez_ref, hz_ref, ci_ref, None)
        out(j + 1).start()
    for j in range(depth + 1):
        out(j).wait()


def forward_body(tile_ref, perm_ref, e0_ref, h0_ref, up_ref, dn_ref, hist_ref, efin_ref, sum_ref, ci_ref, h_ref, e_ref, ahat_ref, ez_ref, hz_ref, sem):
    sh = Shifts()
    tile = tile_ref[0]
    depth = STEPS

    def fetch(j):
        return pltpu.make_async_copy(hist_ref.at[j], ahat_ref.at[j], sem.at[j])

    for t in range(STEPS):
        fetch(STEPS - 1 - t).start()
    fill_inverse(perm_ref, ci_ref)

    def put(a, c, place, t):
        if a == 1:
            store(h_ref, (c, place), [x * (1.0 / courant) for x in t])
        else:
            store(e_ref, (c, place), t)

    for c in range(3):
        @pl.loop(0, NX)
        def _(p):
            put(0, c, p + GHOST, widen(e0_ref[0, c, p]))
            put(1, c, p + GHOST, widen(h0_ref[0, c, p]))
    unpack(depth, up_ref, True, put)
    unpack(depth, dn_ref, False, put)

    def e_put(c, p, x):
        e_ref[c, p] = x

    def e_mirror(c):
        e_ref[c, GHOST - 1] = e_ref[c, GHOST]

    for t in range(STEPS):
        fetch(STEPS - 1 - t).wait()

        def use(p, curl, t=t):
            q = p - GHOST
            a = [tiles_of(ahat_ref[STEPS - 1 - t, c, q]) for c in range(3)]
            s = each(lambda x0, y0, x1, y1, x2, y2: x0 * y0 + x1 * y1 + x2 * y2, a[0], curl[0], a[1], curl[1], a[2], curl[2])
            s = joined(s)
            if t > 0:
                s = s + sum_ref[q]
            sum_ref[q] = s

        sweep(sh, tile, depth - t, lambda c, p: e_ref[c, p], e_put, e_mirror, h_ref, ez_ref, hz_ref, ci_ref, use)
    for c in range(3):
        @pl.loop(0, NX)
        def _(p):
            efin_ref[0, c, p] = e_ref[c, p + GHOST][:, :NZ]


VM = pl.BlockSpec(memory_space=pltpu.VMEM)
SM = pl.BlockSpec(memory_space=pltpu.SMEM)
ANY = pl.BlockSpec(memory_space=pl.ANY)
FIELD = (3, ALL, NY, WIDE)


def adjoint(tile, perm, a, b, up, dn, interpret=False):
    return pl.pallas_call(
        adjoint_body,
        out_shape=jax.ShapeDtypeStruct((STEPS, 3, NX, NY, WIDE), F32),
        in_specs=[SM, VM, VM, VM, VM, VM],
        out_specs=ANY,
        scratch_shapes=[
            pltpu.VMEM((ALL, NY, WIDE), F32),
            pltpu.VMEM(FIELD, F32),
            pltpu.VMEM((STEPS, *FIELD), F32),
            pltpu.VMEM((2, ALL, NY, WIDE), F32),
            pltpu.VMEM((2, ALL, NY, WIDE), F32),
            pltpu.SemaphoreType.DMA((STEPS,)),
        ],
        compiler_params=pltpu.CompilerParams(vmem_limit_bytes=36 << 20),
        name="adjoint",
        interpret=interpret,
    )(tile, perm, a, b, up, dn)


def forward(tile, perm, e, h, up, dn, hist, interpret=False):
    return pl.pallas_call(
        forward_body,
        out_shape=(
            jax.ShapeDtypeStruct((1, 3, NX, NY, NZ), F32),
            jax.ShapeDtypeStruct((NX, NY, WIDE), F32),
        ),
        in_specs=[SM, VM, VM, VM, VM, VM, ANY],
        out_specs=(VM, VM),
        scratch_shapes=[
            pltpu.VMEM((ALL, NY, WIDE), F32),
            pltpu.VMEM(FIELD, F32),
            pltpu.VMEM(FIELD, F32),
            pltpu.VMEM((STEPS, 3, NX, NY, WIDE), F32),
            pltpu.VMEM((2, ALL, NY, WIDE), F32),
            pltpu.VMEM((2, ALL, NY, WIDE), F32),
            pltpu.SemaphoreType.DMA((STEPS,)),
        ],
        compiler_params=pltpu.CompilerParams(vmem_limit_bytes=36 << 20),
        name="forward",
        interpret=interpret,
    )(tile, perm, e, h, up, dn, hist)


def on_device(permittivity, e_start, h_start, e_cotangent, h_cotangent):
    tiles, sources = lax.axis_size("tile"), lax.axis_size("src")
    tile = lax.axis_index("tile").astype(jnp.int32).reshape(1)
    upward = [(i, i + 1) for i in range(tiles - 1)]
    downward = [(i + 1, i) for i in range(tiles - 1)]
    near = [(t * sources + s, (t - 1) * sources + s) for t in range(1, tiles) for s in range(DEEP - 1)]
    near += [(t * sources + s, (t + 1) * sources + s) for t in range(tiles - 1) for s in range(NX - DEEP + 1, NX)]

    border = lax.ppermute(permittivity, ("tile", "src"), near)
    a_up, a_dn = pack(STEPS - 1, e_cotangent, h_cotangent, "pack_adjoint")
    a_up = lax.ppermute(a_up, "tile", upward)
    a_dn = lax.ppermute(a_dn, "tile", downward)
    e_up, e_dn = pack(STEPS, e_start, h_start, "pack_forward")
    e_up = lax.ppermute(e_up, "tile", upward)
    e_dn = lax.ppermute(e_dn, "tile", downward)
    both = jnp.concatenate([permittivity, border], axis=0)
    perm = lax.all_to_all(jnp.broadcast_to(both, (sources, *both.shape)), "src", 0, 0, tiled=True)
    hist = adjoint(tile, perm, e_cotangent, h_cotangent, a_up, a_dn)
    e_final, sums = forward(tile, perm, e_start, h_start, e_up, e_dn, hist)
    parts = lax.all_to_all(sums, "src", 0, 0, tiled=True)
    total = jnp.sum(parts, axis=0, keepdims=True)[:, :, :NZ]
    gradient = -(courant * courant) * total / permittivity
    return e_final, gradient


def solution(mesh):
    field = P("src", None, "tile", None, None)
    in_specs = (P(("tile", "src"), None, None), field, field, field, field)
    out_specs = (field, P(("tile", "src"), None, None))
    return jax.shard_map(on_device, mesh=mesh, in_specs=in_specs, out_specs=out_specs, check_vma=False)
```

```python
import jax
import jax.numpy as jnp
from jax import lax
from jax.experimental import pallas as pl
from jax.experimental.pallas import tpu as pltpu
from jax.sharding import PartitionSpec as P


STEPS = 6
courant = 0.57
NX, NY, NZ = 16, 16, 320
WIDE = 384
DEEP = 6
GHOST = 12
ALL = GHOST + NX + 12


F32 = jnp.float32


def plane_list(depth, upward):
    if upward and depth == STEPS:
        return [(2, 1, 0), (2, 2, 0)] + [(a, c, p) for p in range(NX - depth + 1, NX) for a in range(2) for c in range(3)]
    if upward:
        return [(a, c, p) for p in range(NX - depth, NX) for a in range(2) for c in range(3)]
    whole = [(a, c, p) for p in range(depth - 1) for a in range(2) for c in range(3)]
    return whole + [(0, 1, depth - 1), (0, 2, depth - 1)]


def first_half_step(e, h, p, c):
    if c == 1:
        x = e(0, p)
        ahead = jnp.concatenate([x[:, 1:], jnp.zeros((NY, 1), F32)], axis=1) - x
        return h(1, p) - courant * (ahead - (e(2, p + 1) - e(2, p)))
    x = e(0, p)
    ahead = jnp.concatenate([x[1:], jnp.zeros((1, NZ), F32)], axis=0) - x
    return h(2, p) - courant * ((e(1, p + 1) - e(1, p)) - ahead)


def pack_body(depth, e_hbm, h_hbm, up_ref, dn_ref, low_ref, high_ref, sem):
    def edges(upward):
        start, ref = (NX - depth, high_ref) if upward else (0, low_ref)
        return [
            pltpu.make_async_copy(x.at[0, :, pl.ds(start, depth)], ref.at[a], sem.at[2 * upward + a])
            for a, x in enumerate((e_hbm, h_hbm))
        ]

    copies = {upward: edges(upward) for upward in (True, False)}
    for upward in (True, False):
        for copy in copies[upward]:
            copy.start()
    for upward, out in ((True, up_ref), (False, dn_ref)):
        for copy in copies[upward]:
            copy.wait()
        ref, base = (high_ref, NX - depth) if upward else (low_ref, 0)
        at = lambda a: lambda c, p, a=a, ref=ref, base=base: ref[a, c, p - base]
        planes = plane_list(depth, upward)
        for k in range(len(planes) // 2):
            tails = []
            for j in range(2):
                a, c, p = planes[2 * k + j]
                x = first_half_step(at(0), at(1), NX - depth, c) if a == 2 else at(a)(c, p)
                out[k, 2 * j] = x[:, 0:128]
                out[k, 2 * j + 1] = x[:, 128:256]
                tails.append(x[:, 256:320])
            out[k, 4] = jnp.concatenate(tails, axis=1)


def pack(depth, e, h):
    up = len(plane_list(depth, True)) // 2
    dn = len(plane_list(depth, False)) // 2
    return pl.pallas_call(
        lambda *refs: pack_body(depth, *refs),
        out_shape=(
            jax.ShapeDtypeStruct((up, 5, 16, 128), F32),
            jax.ShapeDtypeStruct((dn, 5, 16, 128), F32),
        ),
        in_specs=[HBM] * 2,
        out_specs=[pl.BlockSpec(memory_space=pltpu.VMEM)] * 2,
        scratch_shapes=[
            pltpu.VMEM((2, 3, depth, NY, NZ), F32),
            pltpu.VMEM((2, 3, depth, NY, NZ), F32),
            pltpu.SemaphoreType.DMA((4,)),
        ],
        compiler_params=pltpu.CompilerParams(vmem_limit_bytes=60 << 20),
    )(e, h)


def unpack(depth, buf, upward, put):
    planes = plane_list(depth, upward)
    for k in range(len(planes) // 2):
        tail = buf[k, 4]
        low = lax.broadcasted_iota(jnp.int32, (16, 128), 1) < 64
        tails = (jnp.where(low, tail, 0.0), jnp.where(low, pltpu.roll(tail, 64, 1), 0.0))
        for j in range(2):
            a, c, p = planes[2 * k + j]
            if a == 2:
                put(1, c, GHOST - depth, (buf[k, 2 * j], buf[k, 2 * j + 1], tails[j]))
                continue
            place = p - NX + GHOST if upward else p + NX + GHOST
            put(a, c, place, (buf[k, 2 * j], buf[k, 2 * j + 1], tails[j]))


def widen(x):
    return (x[:, 0:128], x[:, 128:256], jnp.concatenate([x[:, 256:320], jnp.zeros((16, 64), F32)], axis=1))


def store(ref, index, tiles):
    for k in range(3):
        ref[(*index, slice(None), slice(128 * k, 128 * k + 128))] = tiles[k]


def tiles_of(x):
    return [[x[8 * r : 8 * r + 8, 128 * k : 128 * k + 128] for k in range(3)] for r in range(2)]


def joined(v):
    return jnp.concatenate([jnp.concatenate(row, axis=1) for row in v], axis=0)


class Shifts:
    def __init__(self):
        lane = lax.broadcasted_iota(jnp.int32, (8, 128), 1)
        row = lax.broadcasted_iota(jnp.int32, (8, 128), 0)
        self.first_lane, self.last_lane = lane == 0, lane == 127
        self.first_row, self.last_row = row == 0, row == 7

    def ahead_z(self, v):
        out = []
        for r in range(2):
            m = [pltpu.roll(t, 127, 1) for t in v[r]]
            out.append([jnp.where(self.last_lane, m[1], m[0]), jnp.where(self.last_lane, m[2], m[1]), m[2]])
        return out

    def behind_z(self, v):
        out = []
        for r in range(2):
            m = [pltpu.roll(t, 1, 1) for t in v[r]]
            out.append([jnp.where(self.first_lane, 0.0, m[0])] + [jnp.where(self.first_lane, m[k - 1], m[k]) for k in (1, 2)])
        return out

    def ahead_y(self, v):
        m = [[pltpu.roll(t, 7, 0) for t in row] for row in v]
        return [
            [jnp.where(self.last_row, m[1][k], m[0][k]) for k in range(3)],
            [jnp.where(self.last_row, 0.0, m[1][k]) for k in range(3)],
        ]

    def behind_y(self, v):
        m = [[pltpu.roll(t, 1, 0) for t in row] for row in v]
        return [
            [jnp.where(self.first_row, 0.0, m[0][k]) for k in range(3)],
            [jnp.where(self.first_row, m[0][k], m[1][k]) for k in range(3)],
        ]


def each(fn, *vs):
    return [[fn(*(v[r][k] for v in vs)) for k in range(3)] for r in range(2)]


def h_phase(sh, e_at, h_ref, ez_ref, hz_ref, q):
    e = [[tiles_of(e_at(c, q + d)) for c in range(3)] for d in range(2)]
    e.append([None] + [tiles_of(e_at(c, q + 2)) for c in (1, 2)])
    for d in range(2):
        here, then = e[d], e[d + 1]
        z0, z1 = (tiles_of(ez_ref[c, q + d]) for c in range(2))
        y2, y0 = sh.ahead_y(here[2]), sh.ahead_y(here[0])
        h = [tiles_of(h_ref[c, q + d]) for c in range(3)]
        f = lambda h, a, b, c, d: h - ((a - b) - (c - d))
        h = (
            each(f, h[0], y2, here[2], z1, here[1]),
            each(f, h[1], z0, here[0], then[2], here[2]),
            each(f, h[2], then[1], here[1], y0, here[0]),
        )
        for c in range(3):
            h_ref[c, q + d] = joined(h[c])
        for c in range(2):
            hz_ref[c, q + d] = joined(sh.behind_z(h[c]))


def e_phase(sh, e_at, e_put, h_ref, hz_ref, ci_ref, q, use):
    before = [None] + [tiles_of(h_ref[c, q - 1]) for c in (1, 2)]
    f = lambda a, b, c, d: (a - b) - (c - d)
    for d in range(2):
        h = [tiles_of(h_ref[c, q + d]) for c in range(3)]
        z0, z1 = (tiles_of(hz_ref[c, q + d]) for c in range(2))
        y2, y0 = sh.behind_y(h[2]), sh.behind_y(h[0])
        curl = (
            each(f, h[2], y2, h[1], z1),
            each(f, h[0], z0, h[2], before[2]),
            each(f, h[1], before[1], h[0], y0),
        )
        ci = tiles_of(ci_ref[q + d])
        for c in range(3):
            e_put(c, q + d, joined(each(lambda x, k, y: x + k * y, tiles_of(e_at(c, q + d)), ci, curl[c])))
        if use is not None:
            use(q + d, curl)
        before = h


def sweep(sh, tile, reach, e_at, e_put, e_mirror, h_ref, ez_ref, hz_ref, ci_ref, use):
    @pl.when(tile == 0)
    def _():
        for c in (1, 2):
            e_mirror(c)

    def turn(q, fn):
        for d in range(2):
            for c in range(2):
                ez_ref[c, q + 2 + d] = joined(sh.ahead_z(tiles_of(e_at(c, q + 2 + d))))
        h_phase(sh, e_at, h_ref, ez_ref, hz_ref, q)
        e_phase(sh, e_at, e_put, h_ref, hz_ref, ci_ref, q - 2, fn)

    even = reach + reach % 2
    own, end = GHOST, GHOST + NX
    ranges = ((own - even - 2, own + 2, None), (own + 2, end + 2, use), (end + 2, GHOST + NX + reach - 1 + reach % 2 * 1 + 2, None))
    ranges = ranges[:2] + ((end + 2, end + even + 2 if reach % 2 == 0 else end + reach + 1, None),)
    for start, stop, fn in ranges:
        if stop > start:
            @pl.loop(0, (stop - start) // 2)
            def _(i, start=start, fn=fn):
                turn(start + 2 * i, fn)


def stage(refs, *staged):
    copies = [pltpu.make_async_copy(ref, place, staged[-1].at[k]) for k, (ref, place) in enumerate(zip(refs, staged))]
    for copy in copies:
        copy.start()

    def ready(*which):
        for k in which:
            copies[k].wait()

    return (*staged[:-1], ready)


def staging(*arrays):
    return [pltpu.VMEM(x.shape, F32) for x in arrays] + [pltpu.SemaphoreType.DMA((len(arrays),))]


def fill_inverse(perm_ref, ci_ref):
    places = [(s, 0, GHOST + s) for s in range(NX)]
    places += [(s, 1, GHOST + NX + s) for s in range(DEEP - 1)]
    places += [(s, 1, s - NX + GHOST) for s in range(NX - DEEP + 1, NX)]
    for s, which, place in places:
        t = widen(perm_ref[s, which])
        store(ci_ref, (place,), [jnp.where(x > 0, (courant * courant) / jnp.where(x > 0, x, 1.0), 0.0) for x in t])


def adjoint_body(tile_ref, perm_ref, a_ref, b_ref, up_ref, dn_ref, hist_ref, ci_ref, h_ref, e_ref, ez_ref, hz_ref, sem, *staged):
    sh = Shifts()
    tile = tile_ref[0]
    depth = STEPS - 1
    perm_ref, a_ref, b_ref, up_ref, dn_ref, ready = stage((perm_ref, a_ref, b_ref, up_ref, dn_ref), *staged)
    ready(0)
    fill_inverse(perm_ref, ci_ref)
    ready(1, 2)

    def put(a, c, place, t):
        if a == 1:
            store(h_ref, (c, place), [x * (-1.0 / courant) for x in t])
        else:
            ci = ci_ref[place]
            store(e_ref, (0, c, place), [t[k] * ci[:, 128 * k : 128 * k + 128] * (1.0 / (courant * courant)) for k in range(3)])

    for c in range(3):
        @pl.loop(0, NX)
        def _(p):
            put(0, c, p + GHOST, widen(a_ref[0, c, p]))
            put(1, c, p + GHOST, widen(b_ref[0, c, p]))
    ready(3, 4)
    unpack(depth, up_ref, True, put)
    unpack(depth, dn_ref, False, put)

    def out(j):
        return pltpu.make_async_copy(e_ref.at[j, :, pl.ds(GHOST, NX)], hist_ref.at[j], sem.at[j])

    out(0).start()
    for j in range(depth):
        def e_put(c, p, x, j=j):
            e_ref[j + 1, c, p] = x

        def e_mirror(c, j=j):
            e_ref[j, c, GHOST - 1] = e_ref[j, c, GHOST]

        sweep(sh, tile, depth - j, lambda c, p, j=j: e_ref[j, c, p], e_put, e_mirror, h_ref, ez_ref, hz_ref, ci_ref, None)
        out(j + 1).start()
    for j in range(depth + 1):
        out(j).wait()


def forward_body(tile_ref, perm_ref, e0_ref, h0_ref, up_ref, dn_ref, hist_ref, efin_ref, sum_ref, ci_ref, h_ref, e_ref, ahat_ref, ez_ref, hz_ref, sem, *staged):
    sh = Shifts()
    tile = tile_ref[0]
    depth = STEPS

    def fetch(j):
        return pltpu.make_async_copy(hist_ref.at[j], ahat_ref.at[j], sem.at[j])

    perm_ref, e0_ref, h0_ref, up_ref, dn_ref, ready = stage((perm_ref, e0_ref, h0_ref, up_ref, dn_ref), *staged)
    for t in range(STEPS):
        fetch(STEPS - 1 - t).start()
    ready(0)
    fill_inverse(perm_ref, ci_ref)
    ready(1, 2)

    def put(a, c, place, t):
        if a == 1:
            store(h_ref, (c, place), [x * (1.0 / courant) for x in t])
        else:
            store(e_ref, (c, place), t)

    for c in range(3):
        @pl.loop(0, NX)
        def _(p):
            put(0, c, p + GHOST, widen(e0_ref[0, c, p]))
            put(1, c, p + GHOST, widen(h0_ref[0, c, p]))
    ready(3, 4)
    unpack(depth, up_ref, True, put)
    unpack(depth, dn_ref, False, put)
    last = GHOST - depth
    e_ref[0, last] = jnp.zeros((NY, WIDE), F32)
    for c in (1, 2):
        e_ref[c, last] = e_ref[c, last + 1]

    def e_put(c, p, x):
        e_ref[c, p] = x

    def e_mirror(c):
        e_ref[c, GHOST - 1] = e_ref[c, GHOST]

    for t in range(STEPS):
        fetch(STEPS - 1 - t).wait()

        def use(p, curl, t=t):
            q = p - GHOST
            a = [tiles_of(ahat_ref[STEPS - 1 - t, c, q]) for c in range(3)]
            s = each(lambda x0, y0, x1, y1, x2, y2: x0 * y0 + x1 * y1 + x2 * y2, a[0], curl[0], a[1], curl[1], a[2], curl[2])
            s = joined(s)
            if t > 0:
                s = s + sum_ref[q]
            sum_ref[q] = s

        sweep(sh, tile, depth - t, lambda c, p: e_ref[c, p], e_put, e_mirror, h_ref, ez_ref, hz_ref, ci_ref, use)
    for c in range(3):
        @pl.loop(0, NX)
        def _(p):
            efin_ref[0, c, p] = e_ref[c, p + GHOST][:, :NZ]


VM = pl.BlockSpec(memory_space=pltpu.VMEM)
HBM = pl.BlockSpec(memory_space=pltpu.HBM)
SM = pl.BlockSpec(memory_space=pltpu.SMEM)
FIELD = (3, ALL, NY, WIDE)


def adjoint(tile, perm, a, b, up, dn, interpret=False):
    return pl.pallas_call(
        adjoint_body,
        out_shape=jax.ShapeDtypeStruct((STEPS, 3, NX, NY, WIDE), F32),
        in_specs=[SM] + [HBM] * 5,
        out_specs=HBM,
        scratch_shapes=[
            pltpu.VMEM((ALL, NY, WIDE), F32),
            pltpu.VMEM(FIELD, F32),
            pltpu.VMEM((STEPS, *FIELD), F32),
            pltpu.VMEM((2, ALL, NY, WIDE), F32),
            pltpu.VMEM((2, ALL, NY, WIDE), F32),
            pltpu.SemaphoreType.DMA((STEPS,)),
            *staging(perm, a, b, up, dn),
        ],
        compiler_params=pltpu.CompilerParams(vmem_limit_bytes=44 << 20),
        name="adjoint",
        interpret=interpret,
    )(tile, perm, a, b, up, dn)


def forward(tile, perm, e, h, up, dn, hist, interpret=False):
    return pl.pallas_call(
        forward_body,
        out_shape=(
            jax.ShapeDtypeStruct((1, 3, NX, NY, NZ), F32),
            jax.ShapeDtypeStruct((NX, NY, WIDE), F32),
        ),
        in_specs=[SM] + [HBM] * 6,
        out_specs=(VM, VM),
        scratch_shapes=[
            pltpu.VMEM((ALL, NY, WIDE), F32),
            pltpu.VMEM(FIELD, F32),
            pltpu.VMEM(FIELD, F32),
            pltpu.VMEM((STEPS, 3, NX, NY, WIDE), F32),
            pltpu.VMEM((2, ALL, NY, WIDE), F32),
            pltpu.VMEM((2, ALL, NY, WIDE), F32),
            pltpu.SemaphoreType.DMA((STEPS,)),
            *staging(perm, e, h, up, dn),
        ],
        compiler_params=pltpu.CompilerParams(vmem_limit_bytes=44 << 20),
        name="forward",
        interpret=interpret,
    )(tile, perm, e, h, up, dn, hist)


def on_device(permittivity, e_start, h_start, e_cotangent, h_cotangent):
    tiles, sources = lax.axis_size("tile"), lax.axis_size("src")
    tile = lax.axis_index("tile").astype(jnp.int32).reshape(1)
    upward = [(i, i + 1) for i in range(tiles - 1)]
    downward = [(i + 1, i) for i in range(tiles - 1)]
    near = [(t * sources + s, (t - 1) * sources + s) for t in range(1, tiles) for s in range(DEEP - 1)]
    near += [(t * sources + s, (t + 1) * sources + s) for t in range(tiles - 1) for s in range(NX - DEEP + 1, NX)]

    border = lax.ppermute(permittivity, ("tile", "src"), near)
    a_up, a_dn = pack(STEPS - 1, e_cotangent, h_cotangent)
    a_up = lax.ppermute(a_up, "tile", upward)
    a_dn = lax.ppermute(a_dn, "tile", downward)
    both = jnp.concatenate([permittivity, border], axis=0)
    perm = lax.all_to_all(jnp.broadcast_to(both, (sources, *both.shape)), "src", 0, 0, tiled=True)
    e_up, e_dn = pack(STEPS, e_start, h_start)
    e_up = lax.ppermute(e_up, "tile", upward)
    e_dn = lax.ppermute(e_dn, "tile", downward)
    hist = adjoint(tile, perm, e_cotangent, h_cotangent, a_up, a_dn)
    e_final, sums = forward(tile, perm, e_start, h_start, e_up, e_dn, hist)
    parts = lax.all_to_all(sums, "src", 0, 0, tiled=True)
    total = jnp.sum(parts, axis=0, keepdims=True)[:, :, :NZ]
    gradient = -(courant * courant) * total / permittivity
    return e_final, gradient


def solution(mesh):
    field = P("src", None, "tile", None, None)
    in_specs = (P(("tile", "src"), None, None), field, field, field, field)
    out_specs = (field, P(("tile", "src"), None, None))

    return jax.shard_map(on_device, mesh=mesh, in_specs=in_specs, out_specs=out_specs, check_vma=False)
```

```python
import jax
import jax.numpy as jnp
from jax import lax
from jax.experimental import pallas as pl
from jax.experimental.pallas import tpu as pltpu
from jax.sharding import PartitionSpec as P


STEPS = 6
courant = 0.57
NX, NY, NZ = 16, 16, 320
WIDE = 384
DEEP = 6
GHOST = 12
ALL = GHOST + NX + 12


F32 = jnp.float32


def plane_list(depth, upward):
    if upward and depth == STEPS:
        return [(2, 1, 0), (2, 2, 0)] + [(a, c, p) for p in range(NX - depth + 1, NX) for a in range(2) for c in range(3)]
    if upward:
        return [(a, c, p) for p in range(NX - depth, NX) for a in range(2) for c in range(3)]
    whole = [(a, c, p) for p in range(depth - 1) for a in range(2) for c in range(3)]
    return whole + [(0, 1, depth - 1), (0, 2, depth - 1)]


def first_half_step(e, h, p, c):
    if c == 1:
        x = e(0, p)
        ahead = jnp.concatenate([x[:, 1:], jnp.zeros((NY, 1), F32)], axis=1) - x
        return h(1, p) - courant * (ahead - (e(2, p + 1) - e(2, p)))
    x = e(0, p)
    ahead = jnp.concatenate([x[1:], jnp.zeros((1, NZ), F32)], axis=0) - x
    return h(2, p) - courant * ((e(1, p + 1) - e(1, p)) - ahead)


def pack_body(depth, e_hbm, h_hbm, up_ref, dn_ref, low_ref, high_ref, sem):
    def edges(upward):
        start, ref = (NX - depth, high_ref) if upward else (0, low_ref)
        return [
            pltpu.make_async_copy(x.at[0, :, pl.ds(start, depth)], ref.at[a], sem.at[2 * upward + a])
            for a, x in enumerate((e_hbm, h_hbm))
        ]

    copies = {upward: edges(upward) for upward in (True, False)}
    for upward in (True, False):
        for copy in copies[upward]:
            copy.start()
    for upward, out in ((True, up_ref), (False, dn_ref)):
        for copy in copies[upward]:
            copy.wait()
        ref, base = (high_ref, NX - depth) if upward else (low_ref, 0)
        at = lambda a: lambda c, p, a=a, ref=ref, base=base: ref[a, c, p - base]
        planes = plane_list(depth, upward)
        for k in range(len(planes) // 2):
            tails = []
            for j in range(2):
                a, c, p = planes[2 * k + j]
                x = first_half_step(at(0), at(1), NX - depth, c) if a == 2 else at(a)(c, p)
                out[k, 2 * j] = x[:, 0:128]
                out[k, 2 * j + 1] = x[:, 128:256]
                tails.append(x[:, 256:320])
            out[k, 4] = jnp.concatenate(tails, axis=1)


def pack(depth, e, h):
    up = len(plane_list(depth, True)) // 2
    dn = len(plane_list(depth, False)) // 2
    return pl.pallas_call(
        lambda *refs: pack_body(depth, *refs),
        out_shape=(
            jax.ShapeDtypeStruct((up, 5, 16, 128), F32),
            jax.ShapeDtypeStruct((dn, 5, 16, 128), F32),
        ),
        in_specs=[HBM] * 2,
        out_specs=[pl.BlockSpec(memory_space=pltpu.VMEM)] * 2,
        scratch_shapes=[
            pltpu.VMEM((2, 3, depth, NY, NZ), F32),
            pltpu.VMEM((2, 3, depth, NY, NZ), F32),
            pltpu.SemaphoreType.DMA((4,)),
        ],
        compiler_params=pltpu.CompilerParams(vmem_limit_bytes=60 << 20),
    )(e, h)


def unpack(depth, buf, upward, put):
    planes = plane_list(depth, upward)
    for k in range(len(planes) // 2):
        tail = buf[k, 4]
        low = lax.broadcasted_iota(jnp.int32, (16, 128), 1) < 64
        tails = (jnp.where(low, tail, 0.0), jnp.where(low, pltpu.roll(tail, 64, 1), 0.0))
        for j in range(2):
            a, c, p = planes[2 * k + j]
            if a == 2:
                put(1, c, GHOST - depth, (buf[k, 2 * j], buf[k, 2 * j + 1], tails[j]))
                continue
            place = p - NX + GHOST if upward else p + NX + GHOST
            put(a, c, place, (buf[k, 2 * j], buf[k, 2 * j + 1], tails[j]))


def widen(x):
    return (x[:, 0:128], x[:, 128:256], jnp.concatenate([x[:, 256:320], jnp.zeros((16, 64), F32)], axis=1))


def store(ref, index, tiles):
    for k in range(3):
        ref[(*index, slice(None), slice(128 * k, 128 * k + 128))] = tiles[k]


def tiles_of(x):
    return [[x[8 * r : 8 * r + 8, 128 * k : 128 * k + 128] for k in range(3)] for r in range(2)]


def joined(v):
    return jnp.concatenate([jnp.concatenate(row, axis=1) for row in v], axis=0)


class Shifts:
    def __init__(self):
        lane = lax.broadcasted_iota(jnp.int32, (8, 128), 1)
        row = lax.broadcasted_iota(jnp.int32, (8, 128), 0)
        self.first_lane, self.last_lane = lane == 0, lane == 127
        self.first_row, self.last_row = row == 0, row == 7

    def ahead_z(self, v):
        out = []
        for r in range(2):
            m = [pltpu.roll(t, 127, 1) for t in v[r]]
            out.append([jnp.where(self.last_lane, m[1], m[0]), jnp.where(self.last_lane, m[2], m[1]), m[2]])
        return out

    def behind_z(self, v):
        out = []
        for r in range(2):
            m = [pltpu.roll(t, 1, 1) for t in v[r]]
            out.append([jnp.where(self.first_lane, 0.0, m[0])] + [jnp.where(self.first_lane, m[k - 1], m[k]) for k in (1, 2)])
        return out

    def ahead_y(self, v):
        m = [[pltpu.roll(t, 7, 0) for t in row] for row in v]
        return [
            [jnp.where(self.last_row, m[1][k], m[0][k]) for k in range(3)],
            [jnp.where(self.last_row, 0.0, m[1][k]) for k in range(3)],
        ]

    def behind_y(self, v):
        m = [[pltpu.roll(t, 1, 0) for t in row] for row in v]
        return [
            [jnp.where(self.first_row, 0.0, m[0][k]) for k in range(3)],
            [jnp.where(self.first_row, m[0][k], m[1][k]) for k in range(3)],
        ]


def each(fn, *vs):
    return [[fn(*(v[r][k] for v in vs)) for k in range(3)] for r in range(2)]


def h_phase(sh, e_at, h_ref, ez_ref, hz_ref, q):
    e = [[tiles_of(e_at(c, q + d)) for c in range(3)] for d in range(2)]
    e.append([None] + [tiles_of(e_at(c, q + 2)) for c in (1, 2)])
    for d in range(2):
        here, then = e[d], e[d + 1]
        z0, z1 = (tiles_of(ez_ref[c, q + d]) for c in range(2))
        y2, y0 = sh.ahead_y(here[2]), sh.ahead_y(here[0])
        h = [tiles_of(h_ref[c, q + d]) for c in range(3)]
        f = lambda h, a, b, c, d: h - ((a - b) - (c - d))
        h = (
            each(f, h[0], y2, here[2], z1, here[1]),
            each(f, h[1], z0, here[0], then[2], here[2]),
            each(f, h[2], then[1], here[1], y0, here[0]),
        )
        for c in range(3):
            h_ref[c, q + d] = joined(h[c])
        for c in range(2):
            hz_ref[c, q + d] = joined(sh.behind_z(h[c]))


def e_phase(sh, e_at, e_put, h_ref, hz_ref, ci_ref, q, use):
    before = [None] + [tiles_of(h_ref[c, q - 1]) for c in (1, 2)]
    f = lambda a, b, c, d: (a - b) - (c - d)
    for d in range(2):
        h = [tiles_of(h_ref[c, q + d]) for c in range(3)]
        z0, z1 = (tiles_of(hz_ref[c, q + d]) for c in range(2))
        y2, y0 = sh.behind_y(h[2]), sh.behind_y(h[0])
        curl = (
            each(f, h[2], y2, h[1], z1),
            each(f, h[0], z0, h[2], before[2]),
            each(f, h[1], before[1], h[0], y0),
        )
        ci = tiles_of(ci_ref[q + d])
        for c in range(3):
            e_put(c, q + d, joined(each(lambda x, k, y: x + k * y, tiles_of(e_at(c, q + d)), ci, curl[c])))
        if use is not None:
            use(q + d, curl)
        before = h


def sweep(sh, tile, reach, e_at, e_put, e_mirror, h_ref, ez_ref, hz_ref, ci_ref, use):
    @pl.when(tile == 0)
    def _():
        for c in (1, 2):
            e_mirror(c)

    def turn(q, fn):
        for d in range(2):
            for c in range(2):
                ez_ref[c, q + 2 + d] = joined(sh.ahead_z(tiles_of(e_at(c, q + 2 + d))))
        h_phase(sh, e_at, h_ref, ez_ref, hz_ref, q)
        e_phase(sh, e_at, e_put, h_ref, hz_ref, ci_ref, q - 2, fn)

    even = reach + reach % 2
    own, end = GHOST, GHOST + NX
    ranges = ((own - even - 2, own + 2, None), (own + 2, end + 2, use), (end + 2, GHOST + NX + reach - 1 + reach % 2 * 1 + 2, None))
    ranges = ranges[:2] + ((end + 2, end + even + 2 if reach % 2 == 0 else end + reach + 1, None),)
    for start, stop, fn in ranges:
        if stop > start:
            @pl.loop(0, (stop - start) // 2)
            def _(i, start=start, fn=fn):
                turn(start + 2 * i, fn)


def stage(refs, *staged):
    copies = [pltpu.make_async_copy(ref, place, staged[-1].at[k]) for k, (ref, place) in enumerate(zip(refs, staged))]
    for copy in copies:
        copy.start()

    def ready(*which):
        for k in which:
            copies[k].wait()

    return (*staged[:-1], ready)


def staging(*arrays):
    return [pltpu.VMEM(x.shape, F32) for x in arrays] + [pltpu.SemaphoreType.DMA((len(arrays),))]


def fill_inverse(perm_ref, ci_ref):
    places = [(s, 0, GHOST + s) for s in range(NX)]
    places += [(s, 1, GHOST + NX + s) for s in range(DEEP - 1)]
    places += [(s, 1, s - NX + GHOST) for s in range(NX - DEEP + 1, NX)]
    for s, which, place in places:
        t = widen(perm_ref[s, which])
        store(ci_ref, (place,), [jnp.where(x > 0, (courant * courant) / jnp.where(x > 0, x, 1.0), 0.0) for x in t])


def adjoint_body(tile_ref, perm_ref, a_ref, b_ref, up_ref, dn_ref, hist_ref, ci_ref, h_ref, e_ref, ez_ref, hz_ref, sem, *staged):
    sh = Shifts()
    tile = tile_ref[0]
    depth = STEPS - 1
    up_ref, dn_ref, ready = stage((up_ref, dn_ref), *staged)
    fill_inverse(perm_ref, ci_ref)

    def put(a, c, place, t):
        if a == 1:
            store(h_ref, (c, place), [x * (-1.0 / courant) for x in t])
        else:
            ci = ci_ref[place]
            store(e_ref, (0, c, place), [t[k] * ci[:, 128 * k : 128 * k + 128] * (1.0 / (courant * courant)) for k in range(3)])

    for c in range(3):
        @pl.loop(0, NX)
        def _(p):
            put(0, c, p + GHOST, widen(a_ref[0, c, p]))
            put(1, c, p + GHOST, widen(b_ref[0, c, p]))
    ready(0, 1)
    unpack(depth, up_ref, True, put)
    unpack(depth, dn_ref, False, put)

    def out(j):
        return pltpu.make_async_copy(e_ref.at[j, :, pl.ds(GHOST, NX)], hist_ref.at[j], sem.at[j])

    out(0).start()
    for j in range(depth):
        def e_put(c, p, x, j=j):
            e_ref[j + 1, c, p] = x

        def e_mirror(c, j=j):
            e_ref[j, c, GHOST - 1] = e_ref[j, c, GHOST]

        sweep(sh, tile, depth - j, lambda c, p, j=j: e_ref[j, c, p], e_put, e_mirror, h_ref, ez_ref, hz_ref, ci_ref, None)
        out(j + 1).start()
    for j in range(depth + 1):
        out(j).wait()


def forward_body(tile_ref, perm_ref, e0_ref, h0_ref, up_ref, dn_ref, hist_ref, efin_ref, sum_ref, ci_ref, h_ref, e_ref, ahat_ref, ez_ref, hz_ref, sem, *staged):
    sh = Shifts()
    tile = tile_ref[0]
    depth = STEPS

    def fetch(j):
        return pltpu.make_async_copy(hist_ref.at[j], ahat_ref.at[j], sem.at[j])

    up_ref, dn_ref, ready = stage((up_ref, dn_ref), *staged)
    for t in range(STEPS):
        fetch(STEPS - 1 - t).start()
    fill_inverse(perm_ref, ci_ref)

    def put(a, c, place, t):
        if a == 1:
            store(h_ref, (c, place), [x * (1.0 / courant) for x in t])
        else:
            store(e_ref, (c, place), t)

    for c in range(3):
        @pl.loop(0, NX)
        def _(p):
            put(0, c, p + GHOST, widen(e0_ref[0, c, p]))
            put(1, c, p + GHOST, widen(h0_ref[0, c, p]))
    ready(0, 1)
    unpack(depth, up_ref, True, put)
    unpack(depth, dn_ref, False, put)
    last = GHOST - depth
    e_ref[0, last] = jnp.zeros((NY, WIDE), F32)
    for c in (1, 2):
        e_ref[c, last] = e_ref[c, last + 1]

    def e_put(c, p, x):
        e_ref[c, p] = x

    def e_mirror(c):
        e_ref[c, GHOST - 1] = e_ref[c, GHOST]

    for t in range(STEPS):
        fetch(STEPS - 1 - t).wait()

        def use(p, curl, t=t):
            q = p - GHOST
            a = [tiles_of(ahat_ref[STEPS - 1 - t, c, q]) for c in range(3)]
            s = each(lambda x0, y0, x1, y1, x2, y2: x0 * y0 + x1 * y1 + x2 * y2, a[0], curl[0], a[1], curl[1], a[2], curl[2])
            s = joined(s)
            if t > 0:
                s = s + sum_ref[q]
            sum_ref[q] = s

        sweep(sh, tile, depth - t, lambda c, p: e_ref[c, p], e_put, e_mirror, h_ref, ez_ref, hz_ref, ci_ref, use)
    for c in range(3):
        @pl.loop(0, NX)
        def _(p):
            efin_ref[0, c, p] = e_ref[c, p + GHOST][:, :NZ]


VM = pl.BlockSpec(memory_space=pltpu.VMEM)
HBM = pl.BlockSpec(memory_space=pltpu.HBM)
SM = pl.BlockSpec(memory_space=pltpu.SMEM)
FIELD = (3, ALL, NY, WIDE)


def adjoint(tile, perm, a, b, up, dn, interpret=False):
    return pl.pallas_call(
        adjoint_body,
        out_shape=jax.ShapeDtypeStruct((STEPS, 3, NX, NY, WIDE), F32),
        in_specs=[SM, VM, VM, VM, HBM, HBM],
        out_specs=HBM,
        scratch_shapes=[
            pltpu.VMEM((ALL, NY, WIDE), F32),
            pltpu.VMEM(FIELD, F32),
            pltpu.VMEM((STEPS, *FIELD), F32),
            pltpu.VMEM((2, ALL, NY, WIDE), F32),
            pltpu.VMEM((2, ALL, NY, WIDE), F32),
            pltpu.SemaphoreType.DMA((STEPS,)),
            *staging(up, dn),
        ],
        compiler_params=pltpu.CompilerParams(vmem_limit_bytes=44 << 20),
        name="adjoint",
        interpret=interpret,
    )(tile, perm, a, b, up, dn)


def forward(tile, perm, e, h, up, dn, hist, interpret=False):
    return pl.pallas_call(
        forward_body,
        out_shape=(
            jax.ShapeDtypeStruct((1, 3, NX, NY, NZ), F32),
            jax.ShapeDtypeStruct((NX, NY, WIDE), F32),
        ),
        in_specs=[SM, VM, VM, VM, HBM, HBM, HBM],
        out_specs=(VM, VM),
        scratch_shapes=[
            pltpu.VMEM((ALL, NY, WIDE), F32),
            pltpu.VMEM(FIELD, F32),
            pltpu.VMEM(FIELD, F32),
            pltpu.VMEM((STEPS, 3, NX, NY, WIDE), F32),
            pltpu.VMEM((2, ALL, NY, WIDE), F32),
            pltpu.VMEM((2, ALL, NY, WIDE), F32),
            pltpu.SemaphoreType.DMA((STEPS,)),
            *staging(up, dn),
        ],
        compiler_params=pltpu.CompilerParams(vmem_limit_bytes=44 << 20),
        name="forward",
        interpret=interpret,
    )(tile, perm, e, h, up, dn, hist)


def on_device(permittivity, e_start, h_start, e_cotangent, h_cotangent):
    tiles, sources = lax.axis_size("tile"), lax.axis_size("src")
    tile = lax.axis_index("tile").astype(jnp.int32).reshape(1)
    upward = [(i, i + 1) for i in range(tiles - 1)]
    downward = [(i + 1, i) for i in range(tiles - 1)]
    near = [(t * sources + s, (t - 1) * sources + s) for t in range(1, tiles) for s in range(DEEP - 1)]
    near += [(t * sources + s, (t + 1) * sources + s) for t in range(tiles - 1) for s in range(NX - DEEP + 1, NX)]

    border = lax.ppermute(permittivity, ("tile", "src"), near)
    a_up, a_dn = pack(STEPS - 1, e_cotangent, h_cotangent)
    a_up = lax.ppermute(a_up, "tile", upward)
    a_dn = lax.ppermute(a_dn, "tile", downward)
    both = jnp.concatenate([permittivity, border], axis=0)
    perm = lax.all_to_all(jnp.broadcast_to(both, (sources, *both.shape)), "src", 0, 0, tiled=True)
    e_up, e_dn = pack(STEPS, e_start, h_start)
    e_up = lax.ppermute(e_up, "tile", upward)
    e_dn = lax.ppermute(e_dn, "tile", downward)
    hist = adjoint(tile, perm, e_cotangent, h_cotangent, a_up, a_dn)
    e_final, sums = forward(tile, perm, e_start, h_start, e_up, e_dn, hist)
    parts = lax.all_to_all(sums, "src", 0, 0, tiled=True)
    total = jnp.sum(parts, axis=0, keepdims=True)[:, :, :NZ]
    gradient = -(courant * courant) * total / permittivity
    return e_final, gradient


def solution(mesh):
    field = P("src", None, "tile", None, None)
    in_specs = (P(("tile", "src"), None, None), field, field, field, field)
    out_specs = (field, P(("tile", "src"), None, None))

    return jax.shard_map(on_device, mesh=mesh, in_specs=in_specs, out_specs=out_specs, check_vma=False)
```

```python
import jax
import jax.numpy as jnp
from jax import lax
from jax.experimental import pallas as pl
from jax.experimental.pallas import tpu as pltpu
from jax.sharding import PartitionSpec as P


STEPS = 6
courant = 0.57
NX, NY, NZ = 16, 16, 320
WIDE = 384
DEEP = 6
GHOST = 12
ALL = GHOST + NX + 12


F32 = jnp.float32


def plane_list(depth, upward):
    if upward and depth == STEPS:
        return [(2, 1, 0), (2, 2, 0)] + [(a, c, p) for p in range(NX - depth + 1, NX) for a in range(2) for c in range(3)]
    if upward:
        return [(a, c, p) for p in range(NX - depth, NX) for a in range(2) for c in range(3)]
    whole = [(a, c, p) for p in range(depth - 1) for a in range(2) for c in range(3)]
    return whole + [(0, 1, depth - 1), (0, 2, depth - 1)]


def first_half_step(e, h, p, c):
    if c == 1:
        x = e(0, p)
        ahead = jnp.concatenate([x[:, 1:], jnp.zeros((NY, 1), F32)], axis=1) - x
        return h(1, p) - courant * (ahead - (e(2, p + 1) - e(2, p)))
    x = e(0, p)
    ahead = jnp.concatenate([x[1:], jnp.zeros((1, NZ), F32)], axis=0) - x
    return h(2, p) - courant * ((e(1, p + 1) - e(1, p)) - ahead)


def pack_body(depth, e_hbm, h_hbm, up_ref, dn_ref, low_ref, high_ref, sem):
    def edges(upward):
        start, ref = (NX - depth, high_ref) if upward else (0, low_ref)
        return [
            pltpu.make_async_copy(x.at[0, :, pl.ds(start, depth)], ref.at[a], sem.at[2 * upward + a])
            for a, x in enumerate((e_hbm, h_hbm))
        ]

    copies = {upward: edges(upward) for upward in (True, False)}
    for upward in (True, False):
        for copy in copies[upward]:
            copy.start()
    for upward, out in ((True, up_ref), (False, dn_ref)):
        for copy in copies[upward]:
            copy.wait()
        ref, base = (high_ref, NX - depth) if upward else (low_ref, 0)
        at = lambda a: lambda c, p, a=a, ref=ref, base=base: ref[a, c, p - base]
        planes = plane_list(depth, upward)
        for k in range(len(planes) // 2):
            tails = []
            for j in range(2):
                a, c, p = planes[2 * k + j]
                x = first_half_step(at(0), at(1), NX - depth, c) if a == 2 else at(a)(c, p)
                out[k, 2 * j] = x[:, 0:128]
                out[k, 2 * j + 1] = x[:, 128:256]
                tails.append(x[:, 256:320])
            out[k, 4] = jnp.concatenate(tails, axis=1)


def pack(depth, e, h):
    up = len(plane_list(depth, True)) // 2
    dn = len(plane_list(depth, False)) // 2
    return pl.pallas_call(
        lambda *refs: pack_body(depth, *refs),
        out_shape=(
            jax.ShapeDtypeStruct((up, 5, 16, 128), F32),
            jax.ShapeDtypeStruct((dn, 5, 16, 128), F32),
        ),
        in_specs=[HBM] * 2,
        out_specs=[pl.BlockSpec(memory_space=pltpu.VMEM)] * 2,
        scratch_shapes=[
            pltpu.VMEM((2, 3, depth, NY, NZ), F32),
            pltpu.VMEM((2, 3, depth, NY, NZ), F32),
            pltpu.SemaphoreType.DMA((4,)),
        ],
        compiler_params=pltpu.CompilerParams(vmem_limit_bytes=60 << 20),
    )(e, h)


def unpack(depth, buf, upward, put):
    planes = plane_list(depth, upward)
    for k in range(len(planes) // 2):
        tail = buf[k, 4]
        low = lax.broadcasted_iota(jnp.int32, (16, 128), 1) < 64
        tails = (jnp.where(low, tail, 0.0), jnp.where(low, pltpu.roll(tail, 64, 1), 0.0))
        for j in range(2):
            a, c, p = planes[2 * k + j]
            if a == 2:
                put(1, c, GHOST - depth, (buf[k, 2 * j], buf[k, 2 * j + 1], tails[j]))
                continue
            place = p - NX + GHOST if upward else p + NX + GHOST
            put(a, c, place, (buf[k, 2 * j], buf[k, 2 * j + 1], tails[j]))


def widen(x):
    return (x[:, 0:128], x[:, 128:256], jnp.concatenate([x[:, 256:320], jnp.zeros((16, 64), F32)], axis=1))


def store(ref, index, tiles):
    for k in range(3):
        ref[(*index, slice(None), slice(128 * k, 128 * k + 128))] = tiles[k]


def tiles_of(x):
    return [[x[8 * r : 8 * r + 8, 128 * k : 128 * k + 128] for k in range(3)] for r in range(2)]


def joined(v):
    return jnp.concatenate([jnp.concatenate(row, axis=1) for row in v], axis=0)


class Shifts:
    def __init__(self):
        lane = lax.broadcasted_iota(jnp.int32, (8, 128), 1)
        row = lax.broadcasted_iota(jnp.int32, (8, 128), 0)
        self.first_lane, self.last_lane = lane == 0, lane == 127
        self.first_row, self.last_row = row == 0, row == 7

    def ahead_z(self, v):
        out = []
        for r in range(2):
            m = [pltpu.roll(t, 127, 1) for t in v[r]]
            out.append([jnp.where(self.last_lane, m[1], m[0]), jnp.where(self.last_lane, m[2], m[1]), m[2]])
        return out

    def behind_z(self, v):
        out = []
        for r in range(2):
            m = [pltpu.roll(t, 1, 1) for t in v[r]]
            out.append([jnp.where(self.first_lane, 0.0, m[0])] + [jnp.where(self.first_lane, m[k - 1], m[k]) for k in (1, 2)])
        return out

    def ahead_y(self, v):
        m = [[pltpu.roll(t, 7, 0) for t in row] for row in v]
        return [
            [jnp.where(self.last_row, m[1][k], m[0][k]) for k in range(3)],
            [jnp.where(self.last_row, 0.0, m[1][k]) for k in range(3)],
        ]

    def behind_y(self, v):
        m = [[pltpu.roll(t, 1, 0) for t in row] for row in v]
        return [
            [jnp.where(self.first_row, 0.0, m[0][k]) for k in range(3)],
            [jnp.where(self.first_row, m[0][k], m[1][k]) for k in range(3)],
        ]


def each(fn, *vs):
    return [[fn(*(v[r][k] for v in vs)) for k in range(3)] for r in range(2)]


def z_phase(sh, e_at, ez_ref, planes):
    for p in planes:
        for c in range(2):
            ez_ref[c, p] = joined(sh.ahead_z(tiles_of(e_at(c, p))))


def h_phase(sh, e_at, h_ref, ez_ref, hz_ref, q, count=2):
    e = [[tiles_of(e_at(c, q + d)) for c in range(3)] for d in range(count)]
    e.append([None] + [tiles_of(e_at(c, q + count)) for c in (1, 2)])
    for d in range(count):
        here, then = e[d], e[d + 1]
        z0, z1 = (tiles_of(ez_ref[c, q + d]) for c in range(2))
        y2, y0 = sh.ahead_y(here[2]), sh.ahead_y(here[0])
        h = [tiles_of(h_ref[c, q + d]) for c in range(3)]
        f = lambda h, a, b, c, d: h - ((a - b) - (c - d))
        h = (
            each(f, h[0], y2, here[2], z1, here[1]),
            each(f, h[1], z0, here[0], then[2], here[2]),
            each(f, h[2], then[1], here[1], y0, here[0]),
        )
        for c in range(3):
            h_ref[c, q + d] = joined(h[c])
        for c in range(2):
            hz_ref[c, q + d] = joined(sh.behind_z(h[c]))


def e_phase(sh, e_at, e_put, h_ref, hz_ref, ci_at, q, use):
    before = [None] + [tiles_of(h_ref[c, q - 1]) for c in (1, 2)]
    f = lambda a, b, c, d: (a - b) - (c - d)
    for d in range(2):
        h = [tiles_of(h_ref[c, q + d]) for c in range(3)]
        z0, z1 = (tiles_of(hz_ref[c, q + d]) for c in range(2))
        y2, y0 = sh.behind_y(h[2]), sh.behind_y(h[0])
        curl = (
            each(f, h[2], y2, h[1], z1),
            each(f, h[0], z0, h[2], before[2]),
            each(f, h[1], before[1], h[0], y0),
        )
        ci = tiles_of(ci_at(q + d))
        for c in range(3):
            e_put(c, q + d, joined(each(lambda x, k, y: x + k * y, tiles_of(e_at(c, q + d)), ci, curl[c])))
        if use is not None:
            use(q + d, curl)
        before = h


def sweep(sh, tile, reach, e_at, e_put, e_mirror, h_ref, ez_ref, hz_ref, ci_at, use):
    @pl.when(tile == 0)
    def _():
        for c in (1, 2):
            e_mirror(c)

    def turn(q, fn):
        z_phase(sh, e_at, ez_ref, (q + 2, q + 3))
        h_phase(sh, e_at, h_ref, ez_ref, hz_ref, q)
        e_phase(sh, e_at, e_put, h_ref, hz_ref, ci_at, q - 2, fn)

    even = reach + reach % 2
    own, end = GHOST, GHOST + NX
    last = end + even + 2 if reach % 2 == 0 else end + reach + 1
    ranges = ((own - even - 2, own + 2, None), (own + 2, end + 2, use), (end + 2, last, None))
    for start, stop, fn in ranges:
        if stop > start:
            @pl.loop(0, (stop - start) // 2)
            def _(i, start=start, fn=fn):
                turn(start + 2 * i, fn)


def stage(refs, *staged):
    copies = [pltpu.make_async_copy(ref, place, staged[-1].at[k]) for k, (ref, place) in enumerate(zip(refs, staged))]
    for copy in copies:
        copy.start()

    def ready(*which):
        for k in which:
            copies[k].wait()

    return (*staged[:-1], ready)


def staging(*arrays):
    return [pltpu.VMEM(x.shape, F32) for x in arrays] + [pltpu.SemaphoreType.DMA((len(arrays),))]


def fill_inverse(core, mine_ref, other_ref, ci_ref):
    for ref, odd in ((mine_ref, core), (other_ref, 1 - core)):
        for j in range(NX // 2):
            places = [(0, GHOST)]
            if 2 * j < DEEP - 1:
                places.append((1, GHOST + NX))
            if 2 * j + 1 > NX - DEEP:
                places.append((1, GHOST - NX))
            for which, base in places:
                t = widen(ref[j, which])
                t = [jnp.where(x > 0, (courant * courant) / jnp.where(x > 0, x, 1.0), 0.0) for x in t]
                store(ci_ref, (base + 2 * j + odd,), t)


def products(a, curl):
    f = lambda x0, y0, x1, y1, x2, y2: x0 * y0 + x1 * y1 + x2 * y2
    return joined(each(f, a[0], curl[0], a[1], curl[1], a[2], curl[2]))


def interior_body(where_ref, mine_ref, other_ref, e0_ref, h0_ref, e_ref, h_ref, ci_ref, past_ref, ez_ref, hz_ref):
    sh = Shifts()
    fill_inverse(where_ref[1], mine_ref, other_ref, ci_ref)
    for c in range(3):
        @pl.loop(0, NX)
        def _(p):
            store(e_ref, (c, p), widen(e0_ref[0, c, p]))
            store(h_ref, (c, p), [x * (1.0 / courant) for x in widen(h0_ref[0, c, p])])

    e_at = lambda c, p: e_ref[c, p]
    ci_at = lambda p: ci_ref[p + GHOST]

    def e_put(c, p, x):
        e_ref[c, p] = x

    def turn(t):
        def use(p, curl):
            for c in range(3):
                past_ref[t, c, p] = joined(curl[c])

        z_phase(sh, e_at, ez_ref, [t + k for k in range(5)])
        h_phase(sh, e_at, h_ref, ez_ref, hz_ref, t, 1)
        h_phase(sh, e_at, h_ref, ez_ref, hz_ref, t + 1)

        @pl.loop(1, NX // 2 - 1 - t)
        def _(i):
            q = t + 1 + 2 * i
            z_phase(sh, e_at, ez_ref, (q + 2, q + 3))
            h_phase(sh, e_at, h_ref, ez_ref, hz_ref, q)
            e_phase(sh, e_at, e_put, h_ref, hz_ref, ci_at, q - 2, use)

        e_phase(sh, e_at, e_put, h_ref, hz_ref, ci_at, NX - 3 - t, use)

    for t in range(STEPS):
        turn(t)


def adjoint_body(where_ref, ci_ref, a_ref, b_ref, up_ref, dn_ref, past_ref, e_ref, sum_ref, h_ref, ez_ref, hz_ref, *staged):
    sh = Shifts()
    depth = STEPS - 1
    up_ref, dn_ref, ready = stage((up_ref, dn_ref), *staged)

    def put(a, c, place, t):
        if a == 1:
            store(h_ref, (c, place), [x * (-1.0 / courant) for x in t])
        else:
            ci = ci_ref[place]
            store(e_ref, (0, c, place), [t[k] * ci[:, 128 * k : 128 * k + 128] * (1.0 / (courant * courant)) for k in range(3)])

    for c in range(3):
        @pl.loop(0, NX)
        def _(p):
            put(0, c, p + GHOST, widen(a_ref[0, c, p]))
            put(1, c, p + GHOST, widen(b_ref[0, c, p]))
    ready(0, 1)
    unpack(depth, up_ref, True, put)
    unpack(depth, dn_ref, False, put)

    for j in range(depth):
        def e_put(c, p, x, j=j):
            e_ref[j + 1, c, p] = x

        def e_mirror(c, j=j):
            e_ref[j, c, GHOST - 1] = e_ref[j, c, GHOST]

        sweep(sh, where_ref[0], depth - j, lambda c, p, j=j: e_ref[j, c, p], e_put, e_mirror, h_ref, ez_ref, hz_ref, lambda p: ci_ref[p], None)

    for p in (0, NX - 1):
        sum_ref[p] = jnp.zeros((NY, WIDE), F32)
    for t in range(STEPS):
        @pl.loop(0, NX // 2 - 1 - t)
        def _(i, t=t):
            for d in range(2):
                p = t + 1 + 2 * i + d
                s = products([tiles_of(e_ref[depth - t, c, p + GHOST]) for c in range(3)], [tiles_of(past_ref[t, c, p]) for c in range(3)])
                sum_ref[p] = s + sum_ref[p] if t > 0 else s


def forward_body(where_ref, ci_ref, e1_ref, h1_ref, part_ref, up_ref, dn_ref, hist_ref, efin_ref, sum_ref, h_ref, e_ref, acc_ref, ez_ref, hz_ref, *staged):
    sh = Shifts()
    depth = STEPS
    edge = NX // 2 - 1

    up_ref, dn_ref, ready = stage((up_ref, dn_ref), *staged)

    def put(a, c, place, t):
        if a == 1:
            store(h_ref, (c, place), [x * (1.0 / courant) for x in t])
        else:
            store(e_ref, (c, place), t)

    for start in (0, NX - edge):
        @pl.loop(start, start + edge)
        def _(p):
            acc_ref[p + GHOST] = part_ref[p]
            for c in range(3):
                e_ref[c, p + GHOST] = e1_ref[c, p]
                h_ref[c, p + GHOST] = h1_ref[c, p]
    for c in range(3):
        for p in range(DEEP, NX - DEEP):
            efin_ref[0, c, p] = e1_ref[c, p][:, :NZ]
    for p in range(DEEP, NX - DEEP):
        sum_ref[p] = part_ref[p]
    ready(0, 1)
    unpack(depth, up_ref, True, put)
    unpack(depth, dn_ref, False, put)
    last = GHOST - depth
    e_ref[0, last] = jnp.zeros((NY, WIDE), F32)
    for c in (1, 2):
        e_ref[c, last] = e_ref[c, last + 1]

    e_at = lambda c, p: e_ref[c, p]
    ci_at = lambda p: ci_ref[p]

    def e_put(c, p, x):
        e_ref[c, p] = x

    @pl.loop(0, STEPS)
    def _(t):
        @pl.when(where_ref[0] == 0)
        def _():
            for c in (1, 2):
                e_ref[c, GHOST - 1] = e_ref[c, GHOST]

        def use(p, curl):
            a = [tiles_of(hist_ref[STEPS - 1 - t, c, p]) for c in range(3)]
            acc_ref[p] = acc_ref[p] + products(a, curl)

        low, high = GHOST - DEEP + t, GHOST + NX - 1 - t
        Z = lambda base, k: z_phase(sh, e_at, ez_ref, (base + 2 * k, base + 2 * k + 1))
        H = lambda base, k: h_phase(sh, e_at, h_ref, ez_ref, hz_ref, base + 2 * k)
        E = lambda base, k: e_phase(sh, e_at, e_put, h_ref, hz_ref, ci_at, base + 2 * k, use)
        for c in range(2):
            hz_ref[c, low + DEEP] = joined(sh.behind_z(tiles_of(h_ref[c, low + DEEP])))
        Z(low, 0), Z(high, 0), Z(low, 1)
        H(low, 0), Z(high, 1)
        H(high, 0), Z(low, 2)
        H(low, 1), Z(high, 2)
        H(high, 1)
        H(low, 2), E(low + 1, 0)
        H(high, 2), E(high, 0)
        E(low + 1, 1), E(high, 1)
        E(low + 1, 2), E(high, 2)

    for start in (0, NX - DEEP):
        @pl.loop(start, start + DEEP)
        def _(p):
            sum_ref[p] = acc_ref[p + GHOST]
            for c in range(3):
                efin_ref[0, c, p] = e_ref[c, p + GHOST][:, :NZ]


VM = pl.BlockSpec(memory_space=pltpu.VMEM)
HBM = pl.BlockSpec(memory_space=pltpu.HBM)
SM = pl.BlockSpec(memory_space=pltpu.SMEM)
FIELD = (3, ALL, NY, WIDE)
PAIR = (2, ALL, NY, WIDE)
ROOM = 18


def shape(*sizes):
    return jax.ShapeDtypeStruct(sizes, F32)


def params(mib):
    return pltpu.CompilerParams(vmem_limit_bytes=mib << 20)


def interior(where, mine, other, e, h):
    return pl.pallas_call(
        interior_body,
        out_shape=(shape(3, ROOM, NY, WIDE), shape(3, ROOM, NY, WIDE), shape(ALL, NY, WIDE), shape(STEPS, 3, NX, NY, WIDE)),
        in_specs=[SM, VM, VM, VM, VM],
        out_specs=(VM, VM, VM, VM),
        scratch_shapes=[
            pltpu.VMEM((2, ROOM, NY, WIDE), F32),
            pltpu.VMEM((2, ROOM, NY, WIDE), F32),
        ],
        compiler_params=params(20),
        name="interior",
    )(where, mine, other, e, h)


def adjoint(where, ci, a, b, up, dn, past):
    return pl.pallas_call(
        adjoint_body,
        out_shape=(shape(STEPS, *FIELD), shape(NX, NY, WIDE)),
        in_specs=[SM, VM, VM, VM, HBM, HBM, VM],
        out_specs=(VM, VM),
        scratch_shapes=[
            pltpu.VMEM(FIELD, F32),
            pltpu.VMEM(PAIR, F32),
            pltpu.VMEM(PAIR, F32),
            *staging(up, dn),
        ],
        compiler_params=params(18),
        name="adjoint",
    )(where, ci, a, b, up, dn, past)


def forward(where, ci, e1, h1, part, up, dn, hist):
    return pl.pallas_call(
        forward_body,
        out_shape=(shape(1, 3, NX, NY, NZ), shape(NX, NY, WIDE)),
        in_specs=[SM, VM, VM, VM, VM, HBM, HBM, VM],
        out_specs=(VM, VM),
        scratch_shapes=[
            pltpu.VMEM(FIELD, F32),
            pltpu.VMEM(FIELD, F32),
            pltpu.VMEM((ALL, NY, WIDE), F32),
            pltpu.VMEM(PAIR, F32),
            pltpu.VMEM(PAIR, F32),
            *staging(up, dn),
        ],
        compiler_params=params(18),
        name="forward",
    )(where, ci, e1, h1, part, up, dn, hist)


def on_device(permittivity, e_start, h_start, e_cotangent, h_cotangent):
    tiles, sources = lax.axis_size("tile"), lax.axis_size("src")
    where = jnp.stack([lax.axis_index("tile"), lax.axis_index("src") % 2]).astype(jnp.int32)
    upward = [(i, i + 1) for i in range(tiles - 1)]
    downward = [(i + 1, i) for i in range(tiles - 1)]
    near = [(t * sources + s, (t - 1) * sources + s) for t in range(1, tiles) for s in range(DEEP - 1)]
    near += [(t * sources + s, (t + 1) * sources + s) for t in range(tiles - 1) for s in range(NX - DEEP + 1, NX)]

    border = lax.ppermute(permittivity, ("tile", "src"), near)
    a_up, a_dn = pack(STEPS - 1, e_cotangent, h_cotangent)
    a_up = lax.ppermute(a_up, "tile", upward)
    a_dn = lax.ppermute(a_dn, "tile", downward)
    both = jnp.concatenate([permittivity, border], axis=0)
    groups = [list(range(k, sources, 2)) for k in range(2)]
    both = jnp.broadcast_to(both, (sources // 2, *both.shape))
    mine = lax.all_to_all(both, "src", 0, 0, tiled=True, axis_index_groups=groups)
    e_up, e_dn = pack(STEPS, e_start, h_start)
    e_up = lax.ppermute(e_up, "tile", upward)
    e_dn = lax.ppermute(e_dn, "tile", downward)
    other = lax.ppermute(mine, "src", [(s, s ^ 1) for s in range(sources)])
    e1, h1, ci, past = interior(where, mine, other, e_start, h_start)
    hist, part = adjoint(where, ci, e_cotangent, h_cotangent, a_up, a_dn, past)
    e_final, sums = forward(where, ci, e1, h1, part, e_up, e_dn, hist)
    parts = lax.all_to_all(sums, "src", 0, 0, tiled=True)
    total = jnp.sum(parts, axis=0, keepdims=True)[:, :, :NZ]
    gradient = -(courant * courant) * total / permittivity
    return e_final, gradient


def solution(mesh):
    field = P("src", None, "tile", None, None)
    in_specs = (P(("tile", "src"), None, None), field, field, field, field)
    out_specs = (field, P(("tile", "src"), None, None))

    return jax.shard_map(on_device, mesh=mesh, in_specs=in_specs, out_specs=out_specs, check_vma=False)
```

```python
import jax
import jax.numpy as jnp
from jax import lax
from jax.experimental import pallas as pl
from jax.experimental.pallas import tpu as pltpu
from jax.sharding import PartitionSpec as P


STEPS = 6
courant = 0.57
NX, NY, NZ = 16, 16, 320
WIDE = 384
DEEP = 6
GHOST = 12
ALL = GHOST + NX + 12


F32 = jnp.float32


def plane_list(depth, upward):
    if upward and depth == STEPS:
        return [(2, 1, 0), (2, 2, 0)] + [(a, c, p) for p in range(NX - depth + 1, NX) for a in range(2) for c in range(3)]
    if upward:
        return [(a, c, p) for p in range(NX - depth, NX) for a in range(2) for c in range(3)]
    whole = [(a, c, p) for p in range(depth - 1) for a in range(2) for c in range(3)]
    return whole + [(0, 1, depth - 1), (0, 2, depth - 1)]


def first_half_step(e, h, p, c):
    if c == 1:
        x = e(0, p)
        ahead = jnp.concatenate([x[:, 1:], jnp.zeros((NY, 1), F32)], axis=1) - x
        return h(1, p) - courant * (ahead - (e(2, p + 1) - e(2, p)))
    x = e(0, p)
    ahead = jnp.concatenate([x[1:], jnp.zeros((1, NZ), F32)], axis=0) - x
    return h(2, p) - courant * ((e(1, p + 1) - e(1, p)) - ahead)


def pack_body(depth, e_hbm, h_hbm, up_ref, dn_ref, low_ref, high_ref, sem):
    def edges(upward):
        start, ref = (NX - depth, high_ref) if upward else (0, low_ref)
        return [
            pltpu.make_async_copy(x.at[0, :, pl.ds(start, depth)], ref.at[a], sem.at[2 * upward + a])
            for a, x in enumerate((e_hbm, h_hbm))
        ]

    copies = {upward: edges(upward) for upward in (True, False)}
    for upward in (True, False):
        for copy in copies[upward]:
            copy.start()
    for upward, out in ((True, up_ref), (False, dn_ref)):
        for copy in copies[upward]:
            copy.wait()
        ref, base = (high_ref, NX - depth) if upward else (low_ref, 0)
        at = lambda a: lambda c, p, a=a, ref=ref, base=base: ref[a, c, p - base]
        planes = plane_list(depth, upward)
        for k in range(len(planes) // 2):
            tails = []
            for j in range(2):
                a, c, p = planes[2 * k + j]
                x = first_half_step(at(0), at(1), NX - depth, c) if a == 2 else at(a)(c, p)
                out[k, 2 * j] = x[:, 0:128]
                out[k, 2 * j + 1] = x[:, 128:256]
                tails.append(x[:, 256:320])
            out[k, 4] = jnp.concatenate(tails, axis=1)


def pack(depth, e, h):
    up = len(plane_list(depth, True)) // 2
    dn = len(plane_list(depth, False)) // 2
    return pl.pallas_call(
        lambda *refs: pack_body(depth, *refs),
        out_shape=(
            jax.ShapeDtypeStruct((up, 5, 16, 128), F32),
            jax.ShapeDtypeStruct((dn, 5, 16, 128), F32),
        ),
        in_specs=[HBM] * 2,
        out_specs=[pl.BlockSpec(memory_space=pltpu.VMEM)] * 2,
        scratch_shapes=[
            pltpu.VMEM((2, 3, depth, NY, NZ), F32),
            pltpu.VMEM((2, 3, depth, NY, NZ), F32),
            pltpu.SemaphoreType.DMA((4,)),
        ],
        compiler_params=pltpu.CompilerParams(vmem_limit_bytes=60 << 20),
    )(e, h)


def unpack(depth, buf, upward, put):
    planes = plane_list(depth, upward)
    for k in range(len(planes) // 2):
        tail = buf[k, 4]
        low = lax.broadcasted_iota(jnp.int32, (16, 128), 1) < 64
        tails = (jnp.where(low, tail, 0.0), jnp.where(low, pltpu.roll(tail, 64, 1), 0.0))
        for j in range(2):
            a, c, p = planes[2 * k + j]
            if a == 2:
                put(1, c, GHOST - depth, (buf[k, 2 * j], buf[k, 2 * j + 1], tails[j]))
                continue
            place = p - NX + GHOST if upward else p + NX + GHOST
            put(a, c, place, (buf[k, 2 * j], buf[k, 2 * j + 1], tails[j]))


def widen(x):
    return (x[:, 0:128], x[:, 128:256], jnp.concatenate([x[:, 256:320], jnp.zeros((16, 64), F32)], axis=1))


def store(ref, index, tiles):
    for k in range(3):
        ref[(*index, slice(None), slice(128 * k, 128 * k + 128))] = tiles[k]


def tiles_of(x):
    return [[x[8 * r : 8 * r + 8, 128 * k : 128 * k + 128] for k in range(3)] for r in range(2)]


def joined(v):
    return jnp.concatenate([jnp.concatenate(row, axis=1) for row in v], axis=0)


class Shifts:
    def __init__(self):
        lane = lax.broadcasted_iota(jnp.int32, (8, 128), 1)
        row = lax.broadcasted_iota(jnp.int32, (8, 128), 0)
        self.first_lane, self.last_lane = lane == 0, lane == 127
        self.first_row, self.last_row = row == 0, row == 7

    def ahead_z(self, v):
        out = []
        for r in range(2):
            m = [pltpu.roll(t, 127, 1) for t in v[r]]
            out.append([jnp.where(self.last_lane, m[1], m[0]), jnp.where(self.last_lane, m[2], m[1]), m[2]])
        return out

    def behind_z(self, v):
        out = []
        for r in range(2):
            m = [pltpu.roll(t, 1, 1) for t in v[r]]
            out.append([jnp.where(self.first_lane, 0.0, m[0])] + [jnp.where(self.first_lane, m[k - 1], m[k]) for k in (1, 2)])
        return out

    def ahead_y(self, v):
        m = [[pltpu.roll(t, 7, 0) for t in row] for row in v]
        return [
            [jnp.where(self.last_row, m[1][k], m[0][k]) for k in range(3)],
            [jnp.where(self.last_row, 0.0, m[1][k]) for k in range(3)],
        ]

    def behind_y(self, v):
        m = [[pltpu.roll(t, 1, 0) for t in row] for row in v]
        return [
            [jnp.where(self.first_row, 0.0, m[0][k]) for k in range(3)],
            [jnp.where(self.first_row, m[0][k], m[1][k]) for k in range(3)],
        ]


def each(fn, *vs):
    return [[fn(*(v[r][k] for v in vs)) for k in range(3)] for r in range(2)]


def z_phase(sh, e_at, ez_ref, planes):
    for p in planes:
        for c in range(2):
            ez_ref[c, p] = joined(sh.ahead_z(tiles_of(e_at(c, p))))


def h_phase(sh, e_at, h_ref, ez_ref, hz_ref, q, count=2):
    e = [[tiles_of(e_at(c, q + d)) for c in range(3)] for d in range(count)]
    e.append([None] + [tiles_of(e_at(c, q + count)) for c in (1, 2)])
    for d in range(count):
        here, then = e[d], e[d + 1]
        z0, z1 = (tiles_of(ez_ref[c, q + d]) for c in range(2))
        y2, y0 = sh.ahead_y(here[2]), sh.ahead_y(here[0])
        h = [tiles_of(h_ref[c, q + d]) for c in range(3)]
        f = lambda h, a, b, c, d: h - ((a - b) - (c - d))
        h = (
            each(f, h[0], y2, here[2], z1, here[1]),
            each(f, h[1], z0, here[0], then[2], here[2]),
            each(f, h[2], then[1], here[1], y0, here[0]),
        )
        for c in range(3):
            h_ref[c, q + d] = joined(h[c])
        for c in range(2):
            hz_ref[c, q + d] = joined(sh.behind_z(h[c]))


def e_phase(sh, e_at, e_put, h_ref, hz_ref, ci_at, q, use):
    before = [None] + [tiles_of(h_ref[c, q - 1]) for c in (1, 2)]
    f = lambda a, b, c, d: (a - b) - (c - d)
    for d in range(2):
        h = [tiles_of(h_ref[c, q + d]) for c in range(3)]
        z0, z1 = (tiles_of(hz_ref[c, q + d]) for c in range(2))
        y2, y0 = sh.behind_y(h[2]), sh.behind_y(h[0])
        curl = (
            each(f, h[2], y2, h[1], z1),
            each(f, h[0], z0, h[2], before[2]),
            each(f, h[1], before[1], h[0], y0),
        )
        ci = tiles_of(ci_at(q + d))
        for c in range(3):
            e_put(c, q + d, joined(each(lambda x, k, y: x + k * y, tiles_of(e_at(c, q + d)), ci, curl[c])))
        if use is not None:
            use(q + d, curl)
        before = h


def sweep(sh, first, reach, e_at, e_put, e_mirror, h_ref, ez_ref, hz_ref, ci_at, use):
    for c in (1, 2):
        e_mirror(c, jnp.where(first, e_at(c, GHOST), e_at(c, GHOST - 1)))
    low = GHOST - reach
    pairs = NX // 2 - 1 + reach
    z_phase(sh, e_at, ez_ref, range(low, low + 5))
    h_phase(sh, e_at, h_ref, ez_ref, hz_ref, low, 1)
    h_phase(sh, e_at, h_ref, ez_ref, hz_ref, low + 1)

    @pl.loop(1, pairs)
    def _(i):
        q = low + 1 + 2 * i
        z_phase(sh, e_at, ez_ref, (q + 2, q + 3))
        h_phase(sh, e_at, h_ref, ez_ref, hz_ref, q)
        e_phase(sh, e_at, e_put, h_ref, hz_ref, ci_at, q - 2, use)

    e_phase(sh, e_at, e_put, h_ref, hz_ref, ci_at, low - 1 + 2 * pairs, use)


def stage(refs, *staged):
    copies = [pltpu.make_async_copy(ref, place, staged[-1].at[k]) for k, (ref, place) in enumerate(zip(refs, staged))]
    for copy in copies:
        copy.start()

    def ready(*which):
        for k in which:
            copies[k].wait()

    return (*staged[:-1], ready)


def staging(*arrays):
    return [pltpu.VMEM(x.shape, F32) for x in arrays] + [pltpu.SemaphoreType.DMA((len(arrays),))]


def fill_inverse(core, mine_ref, other_ref, ci_ref):
    for ref, odd in ((mine_ref, core), (other_ref, 1 - core)):
        for j in range(NX // 2):
            places = [(0, GHOST)]
            if 2 * j < DEEP - 1:
                places.append((1, GHOST + NX))
            if 2 * j + 1 > NX - DEEP:
                places.append((1, GHOST - NX))
            for which, base in places:
                t = widen(ref[j, which])
                t = [jnp.where(x > 0, (courant * courant) / jnp.where(x > 0, x, 1.0), 0.0) for x in t]
                store(ci_ref, (base + 2 * j + odd,), t)


def products(a, curl):
    f = lambda x0, y0, x1, y1, x2, y2: x0 * y0 + x1 * y1 + x2 * y2
    return joined(each(f, a[0], curl[0], a[1], curl[1], a[2], curl[2]))


def adjoint_body(where_ref, mine_ref, other_ref, a_ref, b_ref, up_ref, dn_ref, e_ref, ci_ref, h_ref, ez_ref, hz_ref, *staged):
    sh = Shifts()
    depth = STEPS - 1
    up_ref, dn_ref, ready = stage((up_ref, dn_ref), *staged)
    fill_inverse(where_ref[1], mine_ref, other_ref, ci_ref)

    def put(a, c, place, t):
        if a == 1:
            store(h_ref, (c, place), [x * (-1.0 / courant) for x in t])
        else:
            ci = ci_ref[place]
            store(e_ref, (0, c, place), [t[k] * ci[:, 128 * k : 128 * k + 128] * (1.0 / (courant * courant)) for k in range(3)])

    @pl.loop(0, NX)
    def _(p):
        for c in range(3):
            put(0, c, p + GHOST, widen(a_ref[0, c, p]))
            put(1, c, p + GHOST, widen(b_ref[0, c, p]))

    ready(0, 1)
    unpack(depth, up_ref, True, put)
    unpack(depth, dn_ref, False, put)
    for j in range(depth):
        def e_put(c, p, x, j=j):
            e_ref[j + 1, c, p] = x

        def e_mirror(c, x, j=j):
            e_ref[j, c, GHOST - 1] = x

        sweep(sh, where_ref[0] == 0, depth - j, lambda c, p, j=j: e_ref[j, c, p], e_put, e_mirror, h_ref, ez_ref, hz_ref, lambda p: ci_ref[p], None)


def forward_body(where_ref, ci_ref, e0_ref, h0_ref, up_ref, dn_ref, hist_ref, efin_ref, sum_ref, h_ref, e_ref, acc_ref, ez_ref, hz_ref, *staged):
    sh = Shifts()
    depth = STEPS
    up_ref, dn_ref, ready = stage((up_ref, dn_ref), *staged)

    def put(a, c, place, t):
        if a == 1:
            store(h_ref, (c, place), [x * (1.0 / courant) for x in t])
        else:
            store(e_ref, (c, place), t)

    @pl.loop(0, NX)
    def _(p):
        for c in range(3):
            put(0, c, p + GHOST, widen(e0_ref[0, c, p]))
            put(1, c, p + GHOST, widen(h0_ref[0, c, p]))

    ready(0, 1)
    unpack(depth, up_ref, True, put)
    unpack(depth, dn_ref, False, put)
    last = GHOST - depth
    e_ref[0, last] = jnp.zeros((NY, WIDE), F32)
    for c in (1, 2):
        e_ref[c, last] = e_ref[c, last + 1]

    def e_mirror(c, x):
        e_ref[c, GHOST - 1] = x

    for t in range(STEPS):
        done = t == STEPS - 1

        def e_put(c, p, x, done=done):
            if done:
                efin_ref[0, c, p - GHOST] = x[:, :NZ]
            else:
                e_ref[c, p] = x

        def use(p, curl, t=t, done=done):
            s = products([tiles_of(hist_ref[STEPS - 1 - t, c, p]) for c in range(3)], curl)
            if t > 0:
                s = s + acc_ref[p]
            if done:
                sum_ref[p - GHOST] = s
            else:
                acc_ref[p] = s

        sweep(sh, where_ref[0] == 0, depth - t, lambda c, p: e_ref[c, p], e_put, e_mirror, h_ref, ez_ref, hz_ref, lambda p: ci_ref[p], use)


VM = pl.BlockSpec(memory_space=pltpu.VMEM)
HBM = pl.BlockSpec(memory_space=pltpu.HBM)
SM = pl.BlockSpec(memory_space=pltpu.SMEM)
FIELD = (3, ALL, NY, WIDE)
PAIR = (2, ALL, NY, WIDE)


def shape(*sizes):
    return jax.ShapeDtypeStruct(sizes, F32)


def params(mib):
    return pltpu.CompilerParams(vmem_limit_bytes=mib << 20)


def adjoint(where, mine, other, a, b, up, dn):
    return pl.pallas_call(
        adjoint_body,
        out_shape=(shape(STEPS, *FIELD), shape(ALL, NY, WIDE)),
        in_specs=[SM, VM, VM, VM, VM, HBM, HBM],
        out_specs=(VM, VM),
        scratch_shapes=[
            pltpu.VMEM(FIELD, F32),
            pltpu.VMEM(PAIR, F32),
            pltpu.VMEM(PAIR, F32),
            *staging(up, dn),
        ],
        compiler_params=params(16),
        name="adjoint",
    )(where, mine, other, a, b, up, dn)


def forward(where, ci, e, h, up, dn, hist):
    return pl.pallas_call(
        forward_body,
        out_shape=(shape(1, 3, NX, NY, NZ), shape(NX, NY, WIDE)),
        in_specs=[SM, VM, VM, VM, HBM, HBM, VM],
        out_specs=(VM, VM),
        scratch_shapes=[
            pltpu.VMEM(FIELD, F32),
            pltpu.VMEM(FIELD, F32),
            pltpu.VMEM((ALL, NY, WIDE), F32),
            pltpu.VMEM(PAIR, F32),
            pltpu.VMEM(PAIR, F32),
            *staging(up, dn),
        ],
        compiler_params=params(20),
        name="forward",
    )(where, ci, e, h, up, dn, hist)


def on_device(permittivity, e_start, h_start, e_cotangent, h_cotangent):
    tiles, sources = lax.axis_size("tile"), lax.axis_size("src")
    where = jnp.stack([lax.axis_index("tile"), lax.axis_index("src") % 2]).astype(jnp.int32)
    upward = [(i, i + 1) for i in range(tiles - 1)]
    downward = [(i + 1, i) for i in range(tiles - 1)]
    near = [(t * sources + s, (t - 1) * sources + s) for t in range(1, tiles) for s in range(DEEP - 1)]
    near += [(t * sources + s, (t + 1) * sources + s) for t in range(tiles - 1) for s in range(NX - DEEP + 1, NX)]

    border = lax.ppermute(permittivity, ("tile", "src"), near)
    a_up, a_dn = pack(STEPS - 1, e_cotangent, h_cotangent)
    a_up = lax.ppermute(a_up, "tile", upward)
    a_dn = lax.ppermute(a_dn, "tile", downward)
    both = jnp.concatenate([permittivity, border], axis=0)
    groups = [list(range(k, sources, 2)) for k in range(2)]
    both = jnp.broadcast_to(both, (sources // 2, *both.shape))
    mine = lax.all_to_all(both, "src", 0, 0, tiled=True, axis_index_groups=groups)
    e_up, e_dn = pack(STEPS, e_start, h_start)
    e_up = lax.ppermute(e_up, "tile", upward)
    e_dn = lax.ppermute(e_dn, "tile", downward)
    other = lax.ppermute(mine, "src", [(s, s ^ 1) for s in range(sources)])
    hist, ci = adjoint(where, mine, other, e_cotangent, h_cotangent, a_up, a_dn)
    e_final, sums = forward(where, ci, e_start, h_start, e_up, e_dn, hist)
    parts = lax.all_to_all(sums, "src", 0, 0, tiled=True)
    total = jnp.sum(parts, axis=0, keepdims=True)[:, :, :NZ]
    gradient = -(courant * courant) * total / permittivity
    return e_final, gradient


def solution(mesh):
    field = P("src", None, "tile", None, None)
    in_specs = (P(("tile", "src"), None, None), field, field, field, field)
    out_specs = (field, P(("tile", "src"), None, None))

    return jax.shard_map(on_device, mesh=mesh, in_specs=in_specs, out_specs=out_specs, check_vma=False)
```

```python
import jax
import jax.numpy as jnp
from jax import lax
from jax.experimental import pallas as pl
from jax.experimental.pallas import tpu as pltpu
from jax.sharding import PartitionSpec as P


STEPS = 6
courant = 0.57
NX, NY, NZ = 16, 16, 320
WIDE = 384
DEEP = 6
GHOST = 12
ALL = GHOST + NX + 12


F32 = jnp.float32


def plane_list(depth, upward):
    if upward and depth == STEPS:
        return [(2, 1, 0), (2, 2, 0)] + [(a, c, p) for p in range(NX - depth + 1, NX) for a in range(2) for c in range(3)]
    if upward:
        return [(a, c, p) for p in range(NX - depth, NX) for a in range(2) for c in range(3)]
    whole = [(a, c, p) for p in range(depth - 1) for a in range(2) for c in range(3)]
    return whole + [(0, 1, depth - 1), (0, 2, depth - 1)]


def first_half_step(e, h, p, c):
    if c == 1:
        x = e(0, p)
        ahead = jnp.concatenate([x[:, 1:], jnp.zeros((NY, 1), F32)], axis=1) - x
        return h(1, p) - courant * (ahead - (e(2, p + 1) - e(2, p)))
    x = e(0, p)
    ahead = jnp.concatenate([x[1:], jnp.zeros((1, NZ), F32)], axis=0) - x
    return h(2, p) - courant * ((e(1, p + 1) - e(1, p)) - ahead)


def pack_body(a_hbm, b_hbm, e_hbm, h_hbm, *refs):
    outs, edges, packed, sem = refs[:4], refs[4:8], refs[8:12], refs[12]
    work = []
    for k, (depth, upward) in enumerate(HALOS):
        start = NX - depth if upward else 0
        fields = (e_hbm, h_hbm) if depth == STEPS else (a_hbm, b_hbm)
        copies = [
            pltpu.make_async_copy(x.at[0, :, pl.ds(start, depth)], edges[k].at[j], sem.at[k, j]) for j, x in enumerate(fields)
        ]
        for copy in copies:
            copy.start()
        work.append((start, copies))
    leaving = []
    for k, (depth, upward) in enumerate(HALOS):
        start, copies = work[k]
        for copy in copies:
            copy.wait()
        at = lambda a: lambda c, p, a=a, ref=edges[k], start=start: ref[a, c, p - start]
        planes = plane_list(depth, upward)
        out = packed[k]
        for i in range(len(planes) // 2):
            tails = []
            for j in range(2):
                a, c, p = planes[2 * i + j]
                x = first_half_step(at(0), at(1), NX - depth, c) if a == 2 else at(a)(c, p)
                out[i, 2 * j] = x[:, 0:128]
                out[i, 2 * j + 1] = x[:, 128:256]
                tails.append(x[:, 256:320])
            out[i, 4] = jnp.concatenate(tails, axis=1)
        copy = pltpu.make_async_copy(out, outs[k], sem.at[k, 2])
        copy.start()
        leaving.append(copy)
    for copy in leaving:
        copy.wait()


HALOS = ((STEPS - 1, True), (STEPS - 1, False), (STEPS, True), (STEPS, False))


def pack(*fields):
    sizes = [(len(plane_list(depth, upward)) // 2, 5, 16, 128) for depth, upward in HALOS]
    return pl.pallas_call(
        pack_body,
        out_shape=[jax.ShapeDtypeStruct(size, F32) for size in sizes],
        in_specs=[HBM] * 4,
        out_specs=[HBM] * 4,
        scratch_shapes=[
            *(pltpu.VMEM((2, 3, depth, NY, NZ), F32) for depth, _ in HALOS),
            *(pltpu.VMEM(size, F32) for size in sizes),
            pltpu.SemaphoreType.DMA((4, 3)),
        ],
        compiler_params=pltpu.CompilerParams(vmem_limit_bytes=60 << 20),
        name="pack",
    )(*fields)


def unpack(depth, buf, upward, put):
    planes = plane_list(depth, upward)
    for k in range(len(planes) // 2):
        tail = buf[k, 4]
        low = lax.broadcasted_iota(jnp.int32, (16, 128), 1) < 64
        tails = (jnp.where(low, tail, 0.0), jnp.where(low, pltpu.roll(tail, 64, 1), 0.0))
        for j in range(2):
            a, c, p = planes[2 * k + j]
            if a == 2:
                put(1, c, GHOST - depth, (buf[k, 2 * j], buf[k, 2 * j + 1], tails[j]))
                continue
            place = p - NX + GHOST if upward else p + NX + GHOST
            put(a, c, place, (buf[k, 2 * j], buf[k, 2 * j + 1], tails[j]))


def widen(x):
    return (x[:, 0:128], x[:, 128:256], jnp.concatenate([x[:, 256:320], jnp.zeros((16, 64), F32)], axis=1))


def store(ref, index, tiles):
    for k in range(3):
        ref[(*index, slice(None), slice(128 * k, 128 * k + 128))] = tiles[k]


def tiles_of(x):
    return [[x[8 * r : 8 * r + 8, 128 * k : 128 * k + 128] for k in range(3)] for r in range(2)]


def joined(v):
    return jnp.concatenate([jnp.concatenate(row, axis=1) for row in v], axis=0)


class Shifts:
    def __init__(self):
        lane = lax.broadcasted_iota(jnp.int32, (8, 128), 1)
        row = lax.broadcasted_iota(jnp.int32, (8, 128), 0)
        self.first_lane, self.last_lane = lane == 0, lane == 127
        self.first_row, self.last_row = row == 0, row == 7

    def ahead_z(self, v):
        out = []
        for r in range(2):
            m = [pltpu.roll(t, 127, 1) for t in v[r]]
            out.append([jnp.where(self.last_lane, m[1], m[0]), jnp.where(self.last_lane, m[2], m[1]), m[2]])
        return out

    def behind_z(self, v):
        out = []
        for r in range(2):
            m = [pltpu.roll(t, 1, 1) for t in v[r]]
            out.append([jnp.where(self.first_lane, 0.0, m[0])] + [jnp.where(self.first_lane, m[k - 1], m[k]) for k in (1, 2)])
        return out

    def ahead_y(self, v):
        m = [[pltpu.roll(t, 7, 0) for t in row] for row in v]
        return [
            [jnp.where(self.last_row, m[1][k], m[0][k]) for k in range(3)],
            [jnp.where(self.last_row, 0.0, m[1][k]) for k in range(3)],
        ]

    def behind_y(self, v):
        m = [[pltpu.roll(t, 1, 0) for t in row] for row in v]
        return [
            [jnp.where(self.first_row, 0.0, m[0][k]) for k in range(3)],
            [jnp.where(self.first_row, m[0][k], m[1][k]) for k in range(3)],
        ]


def each(fn, *vs):
    return [[fn(*(v[r][k] for v in vs)) for k in range(3)] for r in range(2)]


def z_phase(sh, e_at, ez_ref, planes):
    for p in planes:
        for c in range(2):
            ez_ref[c, p] = joined(sh.ahead_z(tiles_of(e_at(c, p))))


def h_phase(sh, e_at, h_ref, ez_ref, hz_ref, q, count=2):
    e = [[tiles_of(e_at(c, q + d)) for c in range(3)] for d in range(count)]
    e.append([None] + [tiles_of(e_at(c, q + count)) for c in (1, 2)])
    for d in range(count):
        here, then = e[d], e[d + 1]
        z0, z1 = (tiles_of(ez_ref[c, q + d]) for c in range(2))
        y2, y0 = sh.ahead_y(here[2]), sh.ahead_y(here[0])
        h = [tiles_of(h_ref[c, q + d]) for c in range(3)]
        f = lambda h, a, b, c, d: h - ((a - b) - (c - d))
        h = (
            each(f, h[0], y2, here[2], z1, here[1]),
            each(f, h[1], z0, here[0], then[2], here[2]),
            each(f, h[2], then[1], here[1], y0, here[0]),
        )
        for c in range(3):
            h_ref[c, q + d] = joined(h[c])
        for c in range(2):
            hz_ref[c, q + d] = joined(sh.behind_z(h[c]))


def e_phase(sh, e_at, e_put, h_ref, hz_ref, ci_at, q, use):
    before = [None] + [tiles_of(h_ref[c, q - 1]) for c in (1, 2)]
    f = lambda a, b, c, d: (a - b) - (c - d)
    for d in range(2):
        h = [tiles_of(h_ref[c, q + d]) for c in range(3)]
        z0, z1 = (tiles_of(hz_ref[c, q + d]) for c in range(2))
        y2, y0 = sh.behind_y(h[2]), sh.behind_y(h[0])
        curl = (
            each(f, h[2], y2, h[1], z1),
            each(f, h[0], z0, h[2], before[2]),
            each(f, h[1], before[1], h[0], y0),
        )
        ci = tiles_of(ci_at(q + d))
        for c in range(3):
            e_put(c, q + d, joined(each(lambda x, k, y: x + k * y, tiles_of(e_at(c, q + d)), ci, curl[c])))
        if use is not None:
            use(q + d, curl)
        before = h


def sweep(sh, first, reach, e_at, e_put, e_mirror, h_ref, ez_ref, hz_ref, ci_at, use):
    for c in (1, 2):
        e_mirror(c, jnp.where(first, e_at(c, GHOST), e_at(c, GHOST - 1)))
    low = GHOST - reach
    pairs = NX // 2 - 1 + reach
    z_phase(sh, e_at, ez_ref, range(low, low + 5))
    h_phase(sh, e_at, h_ref, ez_ref, hz_ref, low, 1)
    h_phase(sh, e_at, h_ref, ez_ref, hz_ref, low + 1)

    @pl.loop(1, pairs)
    def _(i):
        q = low + 1 + 2 * i
        z_phase(sh, e_at, ez_ref, (q + 2, q + 3))
        h_phase(sh, e_at, h_ref, ez_ref, hz_ref, q)
        e_phase(sh, e_at, e_put, h_ref, hz_ref, ci_at, q - 2, use)

    e_phase(sh, e_at, e_put, h_ref, hz_ref, ci_at, low - 1 + 2 * pairs, use)


def stage(refs, *staged):
    copies = [pltpu.make_async_copy(ref, place, staged[-1].at[k]) for k, (ref, place) in enumerate(zip(refs, staged))]
    for copy in copies:
        copy.start()

    def ready(*which):
        for k in which:
            copies[k].wait()

    return (*staged[:-1], ready)


def staging(*arrays):
    return [pltpu.VMEM(x.shape, F32) for x in arrays] + [pltpu.SemaphoreType.DMA((len(arrays),))]


def fill_inverse(core, mine_ref, other_ref, ci_ref):
    for ref, odd in ((mine_ref, core), (other_ref, 1 - core)):
        for j in range(NX // 2):
            places = [(0, GHOST)]
            if 2 * j < DEEP - 1:
                places.append((1, GHOST + NX))
            if 2 * j + 1 > NX - DEEP:
                places.append((1, GHOST - NX))
            for which, base in places:
                t = widen(ref[j, which])
                t = [jnp.where(x > 0, (courant * courant) / jnp.where(x > 0, x, 1.0), 0.0) for x in t]
                store(ci_ref, (base + 2 * j + odd,), t)


def products(a, curl):
    f = lambda x0, y0, x1, y1, x2, y2: x0 * y0 + x1 * y1 + x2 * y2
    return joined(each(f, a[0], curl[0], a[1], curl[1], a[2], curl[2]))


def adjoint_body(where_ref, mine_ref, other_ref, a_ref, b_ref, up_ref, dn_ref, e_ref, ci_ref, h_ref, ez_ref, hz_ref, *staged):
    sh = Shifts()
    depth = STEPS - 1
    up_ref, dn_ref, ready = stage((up_ref, dn_ref), *staged)
    fill_inverse(where_ref[1], mine_ref, other_ref, ci_ref)

    def put(a, c, place, t):
        if a == 1:
            store(h_ref, (c, place), [x * (-1.0 / courant) for x in t])
        else:
            ci = ci_ref[place]
            store(e_ref, (0, c, place), [t[k] * ci[:, 128 * k : 128 * k + 128] * (1.0 / (courant * courant)) for k in range(3)])

    @pl.loop(0, NX)
    def _(p):
        for c in range(3):
            put(0, c, p + GHOST, widen(a_ref[0, c, p]))
            put(1, c, p + GHOST, widen(b_ref[0, c, p]))

    ready(0, 1)
    unpack(depth, up_ref, True, put)
    unpack(depth, dn_ref, False, put)
    for j in range(depth):
        def e_put(c, p, x, j=j):
            e_ref[j + 1, c, p] = x

        def e_mirror(c, x, j=j):
            e_ref[j, c, GHOST - 1] = x

        sweep(sh, where_ref[0] == 0, depth - j, lambda c, p, j=j: e_ref[j, c, p], e_put, e_mirror, h_ref, ez_ref, hz_ref, lambda p: ci_ref[p], None)


def forward_body(where_ref, ci_ref, e0_ref, h0_ref, up_ref, dn_ref, hist_ref, efin_ref, sum_ref, h_ref, e_ref, acc_ref, ez_ref, hz_ref, *staged):
    sh = Shifts()
    depth = STEPS
    up_ref, dn_ref, ready = stage((up_ref, dn_ref), *staged)

    def put(a, c, place, t):
        if a == 1:
            store(h_ref, (c, place), [x * (1.0 / courant) for x in t])
        else:
            store(e_ref, (c, place), t)

    @pl.loop(0, NX)
    def _(p):
        for c in range(3):
            put(0, c, p + GHOST, widen(e0_ref[0, c, p]))
            put(1, c, p + GHOST, widen(h0_ref[0, c, p]))

    ready(0, 1)
    unpack(depth, up_ref, True, put)
    unpack(depth, dn_ref, False, put)
    last = GHOST - depth
    e_ref[0, last] = jnp.zeros((NY, WIDE), F32)
    for c in (1, 2):
        e_ref[c, last] = e_ref[c, last + 1]

    def e_mirror(c, x):
        e_ref[c, GHOST - 1] = x

    for t in range(STEPS):
        done = t == STEPS - 1

        def e_put(c, p, x, done=done):
            if done:
                efin_ref[0, c, p - GHOST] = x[:, :NZ]
            else:
                e_ref[c, p] = x

        def use(p, curl, t=t, done=done):
            s = products([tiles_of(hist_ref[STEPS - 1 - t, c, p]) for c in range(3)], curl)
            if t > 0:
                s = s + acc_ref[p]
            if done:
                sum_ref[p - GHOST] = s
            else:
                acc_ref[p] = s

        sweep(sh, where_ref[0] == 0, depth - t, lambda c, p: e_ref[c, p], e_put, e_mirror, h_ref, ez_ref, hz_ref, lambda p: ci_ref[p], use)


VM = pl.BlockSpec(memory_space=pltpu.VMEM)
HBM = pl.BlockSpec(memory_space=pltpu.HBM)
SM = pl.BlockSpec(memory_space=pltpu.SMEM)
FIELD = (3, ALL, NY, WIDE)
PAIR = (2, ALL, NY, WIDE)


def shape(*sizes):
    return jax.ShapeDtypeStruct(sizes, F32)


def params(mib):
    return pltpu.CompilerParams(vmem_limit_bytes=mib << 20)


def adjoint(where, mine, other, a, b, up, dn):
    return pl.pallas_call(
        adjoint_body,
        out_shape=(shape(STEPS, *FIELD), shape(ALL, NY, WIDE)),
        in_specs=[SM, VM, VM, VM, VM, HBM, HBM],
        out_specs=(VM, VM),
        scratch_shapes=[
            pltpu.VMEM(FIELD, F32),
            pltpu.VMEM(PAIR, F32),
            pltpu.VMEM(PAIR, F32),
            *staging(up, dn),
        ],
        compiler_params=params(16),
        name="adjoint",
    )(where, mine, other, a, b, up, dn)


def forward(where, ci, e, h, up, dn, hist):
    return pl.pallas_call(
        forward_body,
        out_shape=(shape(1, 3, NX, NY, NZ), shape(NX, NY, WIDE)),
        in_specs=[SM, VM, VM, VM, HBM, HBM, VM],
        out_specs=(VM, VM),
        scratch_shapes=[
            pltpu.VMEM(FIELD, F32),
            pltpu.VMEM(FIELD, F32),
            pltpu.VMEM((ALL, NY, WIDE), F32),
            pltpu.VMEM(PAIR, F32),
            pltpu.VMEM(PAIR, F32),
            *staging(up, dn),
        ],
        compiler_params=params(20),
        name="forward",
    )(where, ci, e, h, up, dn, hist)


def on_device(permittivity, e_start, h_start, e_cotangent, h_cotangent):
    tiles, sources = lax.axis_size("tile"), lax.axis_size("src")
    where = jnp.stack([lax.axis_index("tile"), lax.axis_index("src") % 2]).astype(jnp.int32)
    upward = [(i, i + 1) for i in range(tiles - 1)]
    downward = [(i + 1, i) for i in range(tiles - 1)]
    near = [(t * sources + s, (t - 1) * sources + s) for t in range(1, tiles) for s in range(DEEP - 1)]
    near += [(t * sources + s, (t + 1) * sources + s) for t in range(tiles - 1) for s in range(NX - DEEP + 1, NX)]

    border = lax.ppermute(permittivity, ("tile", "src"), near)
    a_up, a_dn, e_up, e_dn = pack(e_cotangent, h_cotangent, e_start, h_start)
    a_up = lax.ppermute(a_up, "tile", upward)
    a_dn = lax.ppermute(a_dn, "tile", downward)
    both = jnp.concatenate([permittivity, border], axis=0)
    groups = [list(range(k, sources, 2)) for k in range(2)]
    both = jnp.broadcast_to(both, (sources // 2, *both.shape))
    mine = lax.all_to_all(both, "src", 0, 0, tiled=True, axis_index_groups=groups)
    e_up = lax.ppermute(e_up, "tile", upward)
    e_dn = lax.ppermute(e_dn, "tile", downward)
    other = lax.ppermute(mine, "src", [(s, s ^ 1) for s in range(sources)])
    hist, ci = adjoint(where, mine, other, e_cotangent, h_cotangent, a_up, a_dn)
    e_final, sums = forward(where, ci, e_start, h_start, e_up, e_dn, hist)
    parts = lax.all_to_all(sums, "src", 0, 0, tiled=True)
    total = jnp.sum(parts, axis=0, keepdims=True)[:, :, :NZ]
    gradient = -(courant * courant) * total / permittivity
    return e_final, gradient


def solution(mesh):
    field = P("src", None, "tile", None, None)
    in_specs = (P(("tile", "src"), None, None), field, field, field, field)
    out_specs = (field, P(("tile", "src"), None, None))

    return jax.shard_map(on_device, mesh=mesh, in_specs=in_specs, out_specs=out_specs, check_vma=False)
```

```python
import jax
import jax.numpy as jnp
from jax import lax
from jax.experimental import pallas as pl
from jax.experimental.pallas import tpu as pltpu
from jax.sharding import PartitionSpec as P


STEPS = 6
courant = 0.57
NX, NY, NZ = 16, 16, 320
WIDE = 384
DEEP = 6
GHOST = 12
ALL = GHOST + NX + 12


F32 = jnp.float32


def plane_list(depth, upward):
    if upward and depth == STEPS:
        return [(2, 1, 0), (2, 2, 0)] + [(a, c, p) for p in range(NX - depth + 1, NX) for a in range(2) for c in range(3)]
    if upward:
        return [(a, c, p) for p in range(NX - depth, NX) for a in range(2) for c in range(3)]
    whole = [(a, c, p) for p in range(depth - 1) for a in range(2) for c in range(3)]
    return whole + [(0, 1, depth - 1), (0, 2, depth - 1)]


def first_half_step(e, h, p, c):
    if c == 1:
        x = e(0, p)
        ahead = jnp.concatenate([x[:, 1:], jnp.zeros((NY, 1), F32)], axis=1) - x
        return h(1, p) - courant * (ahead - (e(2, p + 1) - e(2, p)))
    x = e(0, p)
    ahead = jnp.concatenate([x[1:], jnp.zeros((1, NZ), F32)], axis=0) - x
    return h(2, p) - courant * ((e(1, p + 1) - e(1, p)) - ahead)


def pack_body(a_hbm, b_hbm, e_hbm, h_hbm, *refs):
    outs, edges, packed, sem = refs[:4], refs[4:8], refs[8:12], refs[12]
    work = []
    for k, (depth, upward) in enumerate(HALOS):
        start = NX - depth if upward else 0
        fields = (e_hbm, h_hbm) if depth == STEPS else (a_hbm, b_hbm)
        copies = [
            pltpu.make_async_copy(x.at[0, :, pl.ds(start, depth)], edges[k].at[j], sem.at[k, j]) for j, x in enumerate(fields)
        ]
        for copy in copies:
            copy.start()
        work.append((start, copies))
    leaving = []
    for k, (depth, upward) in enumerate(HALOS):
        start, copies = work[k]
        for copy in copies:
            copy.wait()
        at = lambda a: lambda c, p, a=a, ref=edges[k], start=start: ref[a, c, p - start]
        planes = plane_list(depth, upward)
        out = packed[k]
        for i in range(len(planes) // 2):
            tails = []
            for j in range(2):
                a, c, p = planes[2 * i + j]
                x = first_half_step(at(0), at(1), NX - depth, c) if a == 2 else at(a)(c, p)
                out[i, 2 * j] = x[:, 0:128]
                out[i, 2 * j + 1] = x[:, 128:256]
                tails.append(x[:, 256:320])
            out[i, 4] = jnp.concatenate(tails, axis=1)
        copy = pltpu.make_async_copy(out, outs[k], sem.at[k, 2])
        copy.start()
        leaving.append(copy)
    for copy in leaving:
        copy.wait()


HALOS = ((STEPS - 1, True), (STEPS - 1, False), (STEPS, True), (STEPS, False))


def pack(*fields):
    sizes = [(len(plane_list(depth, upward)) // 2, 5, 16, 128) for depth, upward in HALOS]
    return pl.pallas_call(
        pack_body,
        out_shape=[jax.ShapeDtypeStruct(size, F32) for size in sizes],
        in_specs=[HBM] * 4,
        out_specs=[HBM] * 4,
        scratch_shapes=[
            *(pltpu.VMEM((2, 3, depth, NY, NZ), F32) for depth, _ in HALOS),
            *(pltpu.VMEM(size, F32) for size in sizes),
            pltpu.SemaphoreType.DMA((4, 3)),
        ],
        compiler_params=pltpu.CompilerParams(vmem_limit_bytes=60 << 20),
        name="pack",
    )(*fields)


def unpack(depth, buf, upward, put):
    planes = plane_list(depth, upward)
    for k in range(len(planes) // 2):
        tail = buf[k, 4]
        low = lax.broadcasted_iota(jnp.int32, (16, 128), 1) < 64
        tails = (jnp.where(low, tail, 0.0), jnp.where(low, pltpu.roll(tail, 64, 1), 0.0))
        for j in range(2):
            a, c, p = planes[2 * k + j]
            if a == 2:
                put(1, c, GHOST - depth, (buf[k, 2 * j], buf[k, 2 * j + 1], tails[j]))
                continue
            place = p - NX + GHOST if upward else p + NX + GHOST
            put(a, c, place, (buf[k, 2 * j], buf[k, 2 * j + 1], tails[j]))


def widen(x):
    return (x[:, 0:128], x[:, 128:256], jnp.concatenate([x[:, 256:320], jnp.zeros((16, 64), F32)], axis=1))


def store(ref, index, tiles):
    for k in range(3):
        ref[(*index, slice(None), slice(128 * k, 128 * k + 128))] = tiles[k]


def tiles_of(x):
    return [[x[8 * r : 8 * r + 8, 128 * k : 128 * k + 128] for k in range(3)] for r in range(2)]


def joined(v):
    return jnp.concatenate([jnp.concatenate(row, axis=1) for row in v], axis=0)


class Shifts:
    def __init__(self):
        lane = lax.broadcasted_iota(jnp.int32, (8, 128), 1)
        row = lax.broadcasted_iota(jnp.int32, (8, 128), 0)
        self.first_lane, self.last_lane = lane == 0, lane == 127
        self.first_row, self.last_row = row == 0, row == 7

    def ahead_z(self, v):
        out = []
        for r in range(2):
            m = [pltpu.roll(t, 127, 1) for t in v[r]]
            out.append([jnp.where(self.last_lane, m[1], m[0]), jnp.where(self.last_lane, m[2], m[1]), m[2]])
        return out

    def behind_z(self, v):
        out = []
        for r in range(2):
            m = [pltpu.roll(t, 1, 1) for t in v[r]]
            out.append([jnp.where(self.first_lane, 0.0, m[0])] + [jnp.where(self.first_lane, m[k - 1], m[k]) for k in (1, 2)])
        return out

    def ahead_y(self, v):
        m = [[pltpu.roll(t, 7, 0) for t in row] for row in v]
        return [
            [jnp.where(self.last_row, m[1][k], m[0][k]) for k in range(3)],
            [jnp.where(self.last_row, 0.0, m[1][k]) for k in range(3)],
        ]

    def behind_y(self, v):
        m = [[pltpu.roll(t, 1, 0) for t in row] for row in v]
        return [
            [jnp.where(self.first_row, 0.0, m[0][k]) for k in range(3)],
            [jnp.where(self.first_row, m[0][k], m[1][k]) for k in range(3)],
        ]


def each(fn, *vs):
    return [[fn(*(v[r][k] for v in vs)) for k in range(3)] for r in range(2)]


def z_phase(sh, e_at, ez_ref, planes):
    for p in planes:
        for c in range(2):
            ez_ref[c, p] = joined(sh.ahead_z(tiles_of(e_at(c, p))))


def h_phase(sh, e_at, h_ref, ez_ref, hz_ref, q, count=2):
    e = [[tiles_of(e_at(c, q + d)) for c in range(3)] for d in range(count)]
    e.append([None] + [tiles_of(e_at(c, q + count)) for c in (1, 2)])
    for d in range(count):
        here, then = e[d], e[d + 1]
        z0, z1 = (tiles_of(ez_ref[c, q + d]) for c in range(2))
        y2, y0 = sh.ahead_y(here[2]), sh.ahead_y(here[0])
        h = [tiles_of(h_ref[c, q + d]) for c in range(3)]
        f = lambda h, a, b, c, d: h - ((a - b) - (c - d))
        h = (
            each(f, h[0], y2, here[2], z1, here[1]),
            each(f, h[1], z0, here[0], then[2], here[2]),
            each(f, h[2], then[1], here[1], y0, here[0]),
        )
        for c in range(3):
            h_ref[c, q + d] = joined(h[c])
        for c in range(2):
            hz_ref[c, q + d] = joined(sh.behind_z(h[c]))


def e_phase(sh, e_at, e_put, h_ref, hz_ref, ci_at, q, use):
    before = [None] + [tiles_of(h_ref[c, q - 1]) for c in (1, 2)]
    f = lambda a, b, c, d: (a - b) - (c - d)
    for d in range(2):
        h = [tiles_of(h_ref[c, q + d]) for c in range(3)]
        z0, z1 = (tiles_of(hz_ref[c, q + d]) for c in range(2))
        y2, y0 = sh.behind_y(h[2]), sh.behind_y(h[0])
        curl = (
            each(f, h[2], y2, h[1], z1),
            each(f, h[0], z0, h[2], before[2]),
            each(f, h[1], before[1], h[0], y0),
        )
        ci = tiles_of(ci_at(q + d))
        for c in range(3):
            e_put(c, q + d, joined(each(lambda x, k, y: x + k * y, tiles_of(e_at(c, q + d)), ci, curl[c])))
        if use is not None:
            use(q + d, curl)
        before = h


def sweep(sh, first, reach, e_at, e_put, e_mirror, h_ref, ez_ref, hz_ref, ci_at, use):
    for c in (1, 2):
        e_mirror(c, jnp.where(first, e_at(c, GHOST), e_at(c, GHOST - 1)))
    low = GHOST - reach
    pairs = NX // 2 - 1 + reach
    z_phase(sh, e_at, ez_ref, range(low, low + 5))
    h_phase(sh, e_at, h_ref, ez_ref, hz_ref, low, 1)
    h_phase(sh, e_at, h_ref, ez_ref, hz_ref, low + 1)

    @pl.loop(1, pairs)
    def _(i):
        q = low + 1 + 2 * i
        z_phase(sh, e_at, ez_ref, (q + 2, q + 3))
        h_phase(sh, e_at, h_ref, ez_ref, hz_ref, q)
        e_phase(sh, e_at, e_put, h_ref, hz_ref, ci_at, q - 2, use)

    e_phase(sh, e_at, e_put, h_ref, hz_ref, ci_at, low - 1 + 2 * pairs, use)


def stage(refs, *staged):
    copies = [pltpu.make_async_copy(ref, place, staged[-1].at[k]) for k, (ref, place) in enumerate(zip(refs, staged))]
    for copy in copies:
        copy.start()

    def ready(*which):
        for k in which:
            copies[k].wait()

    return (*staged[:-1], ready)


def staging(*arrays):
    return [pltpu.VMEM(x.shape, F32) for x in arrays] + [pltpu.SemaphoreType.DMA((len(arrays),))]


def fill_inverse(core, mine_ref, other_ref, ci_ref):
    for ref, odd in ((mine_ref, core), (other_ref, 1 - core)):
        for j in range(NX // 2):
            places = [(0, GHOST)]
            if 2 * j < DEEP - 1:
                places.append((1, GHOST + NX))
            if 2 * j + 1 > NX - DEEP:
                places.append((1, GHOST - NX))
            for which, base in places:
                t = widen(ref[j, which])
                t = [jnp.where(x > 0, (courant * courant) / jnp.where(x > 0, x, 1.0), 0.0) for x in t]
                store(ci_ref, (base + 2 * j + odd,), t)


def products(a, curl):
    f = lambda x0, y0, x1, y1, x2, y2: x0 * y0 + x1 * y1 + x2 * y2
    return joined(each(f, a[0], curl[0], a[1], curl[1], a[2], curl[2]))


def adjoint_body(where_ref, mine_ref, other_ref, a_ref, b_ref, up_ref, dn_ref, e_ref, ci_ref, h_ref, ez_ref, hz_ref, *staged):
    sh = Shifts()
    depth = STEPS - 1
    up_ref, dn_ref, ready = stage((up_ref, dn_ref), *staged)
    fill_inverse(where_ref[1], mine_ref, other_ref, ci_ref)

    def put(a, c, place, t):
        if a == 1:
            store(h_ref, (c, place), [x * (-1.0 / courant) for x in t])
        else:
            ci = ci_ref[place]
            store(e_ref, (0, c, place), [t[k] * ci[:, 128 * k : 128 * k + 128] * (1.0 / (courant * courant)) for k in range(3)])

    @pl.loop(0, NX)
    def _(p):
        for c in range(3):
            put(0, c, p + GHOST, widen(a_ref[0, c, p]))
            put(1, c, p + GHOST, widen(b_ref[0, c, p]))

    ready(0, 1)
    unpack(depth, up_ref, True, put)
    unpack(depth, dn_ref, False, put)
    for j in range(depth):
        def e_put(c, p, x, j=j):
            e_ref[j + 1, c, p] = x

        def e_mirror(c, x, j=j):
            e_ref[j, c, GHOST - 1] = x

        sweep(sh, where_ref[0] == 0, depth - j, lambda c, p, j=j: e_ref[j, c, p], e_put, e_mirror, h_ref, ez_ref, hz_ref, lambda p: ci_ref[p], None)


def interior_body(ci_ref, e0_ref, h0_ref, hist_ref, e_ref, h_ref, part_ref, ez_ref, hz_ref):
    sh = Shifts()

    @pl.loop(0, NX)
    def _(p):
        for c in range(3):
            store(e_ref, (c, p), widen(e0_ref[0, c, p]))
            store(h_ref, (c, p), [x * (1.0 / courant) for x in widen(h0_ref[0, c, p])])

    for p in (0, NX - 1):
        part_ref[p] = jnp.zeros((NY, WIDE), F32)
    e_at = lambda c, p: e_ref[c, p]
    ci_at = lambda p: ci_ref[p + GHOST]

    def e_put(c, p, x):
        e_ref[c, p] = x

    for t in range(STEPS):
        def use(p, curl, t=t):
            s = products([tiles_of(hist_ref[STEPS - 1 - t, c, p + GHOST]) for c in range(3)], curl)
            part_ref[p] = s + part_ref[p] if t > 0 else s

        z_phase(sh, e_at, ez_ref, range(t, t + 5))
        h_phase(sh, e_at, h_ref, ez_ref, hz_ref, t, 1)
        h_phase(sh, e_at, h_ref, ez_ref, hz_ref, t + 1)

        @pl.loop(1, NX // 2 - 1 - t)
        def _(i, t=t, use=use):
            q = t + 1 + 2 * i
            z_phase(sh, e_at, ez_ref, (q + 2, q + 3))
            h_phase(sh, e_at, h_ref, ez_ref, hz_ref, q)
            e_phase(sh, e_at, e_put, h_ref, hz_ref, ci_at, q - 2, use)

        e_phase(sh, e_at, e_put, h_ref, hz_ref, ci_at, NX - 3 - t, use)


def forward_body(where_ref, ci_ref, e1_ref, h1_ref, part_ref, up_ref, dn_ref, hist_ref, efin_ref, sum_ref, h_ref, e_ref, acc_ref, ez_ref, hz_ref, *staged):
    sh = Shifts()
    depth = STEPS
    edge = NX // 2 - 1

    up_ref, dn_ref, ready = stage((up_ref, dn_ref), *staged)

    def put(a, c, place, t):
        if a == 1:
            store(h_ref, (c, place), [x * (1.0 / courant) for x in t])
        else:
            store(e_ref, (c, place), t)

    for start in (0, NX - edge):
        @pl.loop(start, start + edge)
        def _(p):
            acc_ref[p + GHOST] = part_ref[p]
            for c in range(3):
                e_ref[c, p + GHOST] = e1_ref[c, p]
                h_ref[c, p + GHOST] = h1_ref[c, p]
    for c in range(3):
        for p in range(DEEP, NX - DEEP):
            efin_ref[0, c, p] = e1_ref[c, p][:, :NZ]
    for p in range(DEEP, NX - DEEP):
        sum_ref[p] = part_ref[p]
    ready(0, 1)
    unpack(depth, up_ref, True, put)
    unpack(depth, dn_ref, False, put)
    last = GHOST - depth
    e_ref[0, last] = jnp.zeros((NY, WIDE), F32)
    for c in (1, 2):
        e_ref[c, last] = e_ref[c, last + 1]

    e_at = lambda c, p: e_ref[c, p]
    ci_at = lambda p: ci_ref[p]

    def e_put(c, p, x):
        e_ref[c, p] = x

    @pl.loop(0, STEPS)
    def _(t):
        @pl.when(where_ref[0] == 0)
        def _():
            for c in (1, 2):
                e_ref[c, GHOST - 1] = e_ref[c, GHOST]

        def use(p, curl):
            a = [tiles_of(hist_ref[STEPS - 1 - t, c, p]) for c in range(3)]
            acc_ref[p] = acc_ref[p] + products(a, curl)

        low, high = GHOST - DEEP + t, GHOST + NX - 1 - t
        Z = lambda base, k: z_phase(sh, e_at, ez_ref, (base + 2 * k, base + 2 * k + 1))
        H = lambda base, k: h_phase(sh, e_at, h_ref, ez_ref, hz_ref, base + 2 * k)
        E = lambda base, k: e_phase(sh, e_at, e_put, h_ref, hz_ref, ci_at, base + 2 * k, use)
        for c in range(2):
            hz_ref[c, low + DEEP] = joined(sh.behind_z(tiles_of(h_ref[c, low + DEEP])))
        Z(low, 0), Z(high, 0), Z(low, 1)
        H(low, 0), Z(high, 1)
        H(high, 0), Z(low, 2)
        H(low, 1), Z(high, 2)
        H(high, 1)
        H(low, 2), E(low + 1, 0)
        H(high, 2), E(high, 0)
        E(low + 1, 1), E(high, 1)
        E(low + 1, 2), E(high, 2)

    for start in (0, NX - DEEP):
        @pl.loop(start, start + DEEP)
        def _(p):
            sum_ref[p] = acc_ref[p + GHOST]
            for c in range(3):
                efin_ref[0, c, p] = e_ref[c, p + GHOST][:, :NZ]


VM = pl.BlockSpec(memory_space=pltpu.VMEM)
HBM = pl.BlockSpec(memory_space=pltpu.HBM)
SM = pl.BlockSpec(memory_space=pltpu.SMEM)
FIELD = (3, ALL, NY, WIDE)
PAIR = (2, ALL, NY, WIDE)
ROOM = 18
LIMITS = (16, 16, 18)


def shape(*sizes):
    return jax.ShapeDtypeStruct(sizes, F32)


def params(mib):
    return pltpu.CompilerParams(vmem_limit_bytes=mib << 20)


def adjoint(where, mine, other, a, b, up, dn):
    return pl.pallas_call(
        adjoint_body,
        out_shape=(shape(STEPS, *FIELD), shape(ALL, NY, WIDE)),
        in_specs=[SM, VM, VM, VM, VM, HBM, HBM],
        out_specs=(VM, VM),
        scratch_shapes=[
            pltpu.VMEM(FIELD, F32),
            pltpu.VMEM(PAIR, F32),
            pltpu.VMEM(PAIR, F32),
            *staging(up, dn),
        ],
        compiler_params=params(LIMITS[0]),
        name="adjoint",
    )(where, mine, other, a, b, up, dn)


def interior(ci, e, h, hist):
    return pl.pallas_call(
        interior_body,
        out_shape=(shape(3, ROOM, NY, WIDE), shape(3, ROOM, NY, WIDE), shape(NX, NY, WIDE)),
        in_specs=[VM, VM, VM, VM],
        out_specs=(VM, VM, VM),
        scratch_shapes=[
            pltpu.VMEM((2, ROOM, NY, WIDE), F32),
            pltpu.VMEM((2, ROOM, NY, WIDE), F32),
        ],
        compiler_params=params(LIMITS[1]),
        name="interior",
    )(ci, e, h, hist)


def forward(where, ci, e1, h1, part, up, dn, hist):
    return pl.pallas_call(
        forward_body,
        out_shape=(shape(1, 3, NX, NY, NZ), shape(NX, NY, WIDE)),
        in_specs=[SM, VM, VM, VM, VM, HBM, HBM, VM],
        out_specs=(VM, VM),
        scratch_shapes=[
            pltpu.VMEM(FIELD, F32),
            pltpu.VMEM(FIELD, F32),
            pltpu.VMEM((ALL, NY, WIDE), F32),
            pltpu.VMEM(PAIR, F32),
            pltpu.VMEM(PAIR, F32),
            *staging(up, dn),
        ],
        compiler_params=params(LIMITS[2]),
        name="forward",
    )(where, ci, e1, h1, part, up, dn, hist)


def on_device(permittivity, e_start, h_start, e_cotangent, h_cotangent):
    tiles, sources = lax.axis_size("tile"), lax.axis_size("src")
    where = jnp.stack([lax.axis_index("tile"), lax.axis_index("src") % 2]).astype(jnp.int32)
    upward = [(i, i + 1) for i in range(tiles - 1)]
    downward = [(i + 1, i) for i in range(tiles - 1)]
    near = [(t * sources + s, (t - 1) * sources + s) for t in range(1, tiles) for s in range(DEEP - 1)]
    near += [(t * sources + s, (t + 1) * sources + s) for t in range(tiles - 1) for s in range(NX - DEEP + 1, NX)]

    border = lax.ppermute(permittivity, ("tile", "src"), near)
    a_up, a_dn, e_up, e_dn = pack(e_cotangent, h_cotangent, e_start, h_start)
    a_up = lax.ppermute(a_up, "tile", upward)
    a_dn = lax.ppermute(a_dn, "tile", downward)
    both = jnp.concatenate([permittivity, border], axis=0)
    groups = [list(range(k, sources, 2)) for k in range(2)]
    both = jnp.broadcast_to(both, (sources // 2, *both.shape))
    mine = lax.all_to_all(both, "src", 0, 0, tiled=True, axis_index_groups=groups)
    e_up = lax.ppermute(e_up, "tile", upward)
    e_dn = lax.ppermute(e_dn, "tile", downward)
    other = lax.ppermute(mine, "src", [(s, s ^ 1) for s in range(sources)])
    hist, ci = adjoint(where, mine, other, e_cotangent, h_cotangent, a_up, a_dn)
    e1, h1, part = interior(ci, e_start, h_start, hist)
    e_final, sums = forward(where, ci, e1, h1, part, e_up, e_dn, hist)
    parts = lax.all_to_all(sums, "src", 0, 0, tiled=True)
    total = jnp.sum(parts, axis=0, keepdims=True)[:, :, :NZ]
    gradient = -(courant * courant) * total / permittivity
    return e_final, gradient


def solution(mesh):
    field = P("src", None, "tile", None, None)
    in_specs = (P(("tile", "src"), None, None), field, field, field, field)
    out_specs = (field, P(("tile", "src"), None, None))

    return jax.shard_map(on_device, mesh=mesh, in_specs=in_specs, out_specs=out_specs, check_vma=False)
```
